128 devices in a mesh: dp: 4 (over x_lo, core), seq: 32 (over y, x_hi, z).
Axes of the slice: x: 4 (x_hi: 2, x_lo: 2; x = x_hi * 2 + x_lo), y: 4, z: 4, core: 2. Of those that a mesh axis runs over, the one named last changes fastest.
Arguments:
- embeddings: bfloat16 [4, 32, 512, 8192], P('dp', 'seq'), may hold values from -6 to 6
- layout: int32 [4, 32, 32], P('dp'), may hold values from 0 to 31, as said below
- lengths: int32 [4], P('dp'), may hold values from 4096 to 16384, as said below
- targets: int32 [4, 4096, 2048], P('dp', 'seq'), may hold values from 0 to 7
- projection: bfloat16 [8192, 768], P('dp'), may hold values from -0.0625 to 0.0625
- kernels: bfloat16 [2, 3, 768, 384], replicated, may hold values from -0.125 to 0.125
- mixers: bfloat16 [2, 384, 768], replicated, may hold values from -0.3125 to 0.3125
- readout: bfloat16 [768, 2048], replicated, may hold values from -0.21875 to 0.21875
Outputs:
- kernel_grads: float32 [2, 3, 768, 384], P(None, None, 'seq', 'dp')
- mixer_grads: float32 [2, 384, 768], P(None, 'seq', 'dp')
- readout_grad: float32 [768, 2048], P('seq', 'dp')
- trunk_grad: float32 [4, 8192, 768], P('dp', 'seq')
The draws below stay inside these ranges and needn't reach their ends.
Inputs may be any that keep to these rules, and one draw needn't show every extreme that they name: For every window w and shard j, layout[w, s, j] over all shards s lists every block number once. `lengths`: multiples of 128; in every draw one window has the full 16384 and another the least.
All inputs are finite; a program needn't handle non-finite values.
Results may differ from the reference program's by a relative error of at most 0.017.
Values may be sent and summed in bfloat16 or wider, within the bound.
A program may use at most 128 MiB of HBM per device.

```python
import math
import jax
import jax.numpy as jnp
from jax import lax

EMB = 8192
CH = 768
INNER = 384
TRACKS = 2048
ROWS_DEV = 512
WINDOWS = 4
POSITIONS = 16384
BINS = 4096
BLOCK = 16
SPREAD_FINE = 256
SPREAD_COARSE = 128
N_SEQ = 32


def draw_layout(key, part):
    keys = jax.random.split(key, WINDOWS * N_SEQ)
    orders = jax.vmap(lambda single: jax.random.permutation(single, N_SEQ))(keys)
    orders = orders.reshape(WINDOWS, N_SEQ, N_SEQ)
    return jnp.transpose(orders, (0, 2, 1)).astype(jnp.int32)


def draw_lengths(key, part):
    first_key, second_key = jax.random.split(key)
    blocks = jax.random.randint(first_key, (WINDOWS,), POSITIONS // 512, POSITIONS // 128 + 1)
    chosen = jax.random.randint(second_key, (), 0, WINDOWS)
    windows_index = jnp.arange(WINDOWS)
    blocks = jnp.where(windows_index == chosen, POSITIONS // 128, blocks)
    blocks = jnp.where(windows_index == (chosen + 1) % WINDOWS, POSITIONS // 512, blocks)
    return (blocks * 128).astype(jnp.int32)


def set_ends(entries, own_key, least, largest):
    dims = entries.shape
    place = [jax.random.randint(jax.random.fold_in(own_key, axis), (), 0, dims[axis]) for axis in range(len(dims))]
    entries = entries.at[tuple(place)].set(least)
    longest = dims.index(max(dims))
    place[longest] = (place[longest] + 1) % dims[longest]
    return entries.at[tuple(place)].set(largest)


def shard_levels(own_key, shape, cuts, least, top_value):
    level = 1.0
    for axis_at, shards_of in cuts:
        draws = jax.random.uniform(jax.random.fold_in(jax.random.fold_in(own_key, 6), axis_at), (shards_of,), jnp.float32, least / len(cuts), top_value / len(cuts))
        level = level * jnp.repeat(jnp.exp(draws), shape[axis_at] // shards_of).reshape((-1,) + (1,) * (len(shape) - 1 - axis_at))
    return level


def gaussian(stream_key, extent, scale, reach, cuts=(), kind=jnp.bfloat16):
    level = shard_levels(stream_key, extent, cuts, -0.22, 0.18) if cuts else 1.0
    drawn = jax.random.normal(stream_key, extent, jnp.float32) * scale * level
    return jnp.minimum(jnp.maximum(drawn, -reach), reach).astype(kind)


def setup_inputs(seed: int = 0) -> dict:
    splits = jax.random.split(jax.random.key(seed), 9)
    return {
        "embeddings": gaussian(splits[0], (WINDOWS, N_SEQ, ROWS_DEV, EMB), 1.0, 6.0, ((0, 4), (1, 32))),
        "layout": draw_layout(jax.random.fold_in(splits[8], 71), 0),
        "lengths": draw_lengths(jax.random.fold_in(splits[8], 71), 0),
        "targets": set_ends(jax.random.randint(splits[3], (WINDOWS, BINS, TRACKS), 0, 8), jax.random.fold_in(splits[3], 1), 0, 7).astype(jnp.int32),
        "projection": gaussian(splits[4], (EMB, CH), EMB ** -0.5, 0.0625, ((0, 4),)),
        "kernels": gaussian(splits[5], (2, 3, CH, INNER), (3 * CH) ** -0.5, 0.125),
        "mixers": gaussian(splits[6], (2, INNER, CH), INNER ** -0.5, 0.3125),
        "readout": gaussian(splits[7], (CH, TRACKS), CH ** -0.5, 0.21875),
    }


def gelu_exact(values):
    return 0.5 * values * (1.0 + lax.erf(values * (1.0 / math.sqrt(2.0))))

def gelu_slope(values):
    cumulative = 0.5 * (1.0 + lax.erf(values * (1.0 / math.sqrt(2.0))))
    density = jnp.exp(-0.5 * values * values) * (1.0 / math.sqrt(2.0 * math.pi))
    return cumulative + values * density

def matmul(left_side, right_side):
    return jnp.dot(left_side, right_side, preferred_element_type=jnp.float32)

def times_transposed(left_side, right_side):
    return lax.dot_general(left_side, right_side, (((1,), (1,)), ((), ())), preferred_element_type=jnp.float32)

def transposed_times(left_side, right_side):
    return lax.dot_general(left_side, right_side, (((0,), (0,)), ((), ())), preferred_element_type=jnp.float32)

def padded_taps(values, spread):
    row_count = values.shape[0]
    padded = jnp.pad(values, ((spread, spread), (0, 0)))
    return (padded[0:row_count], padded[spread:spread + row_count], padded[2 * spread:2 * spread + row_count])

def block_rest(hidden, shifted, kernel, mixing):
    inner_sum = matmul(shifted[0], kernel[0]) + matmul(shifted[1], kernel[1]) + matmul(shifted[2], kernel[2])
    gated_out = gelu_exact(inner_sum).astype(jnp.bfloat16)
    output = hidden.astype(jnp.float32) + matmul(gated_out, mixing)
    pooled = (output.reshape(-1, 2, output.shape[1]).sum(axis=1) * 0.5).astype(jnp.bfloat16)
    return (pooled, inner_sum, gated_out)

def block_backward(upstream, shifted, inner_sum, gated_out, kernel, mixing):
    mixing_grad = transposed_times(gated_out, upstream)
    inner_grad = (times_transposed(upstream, mixing) * gelu_slope(inner_sum)).astype(jnp.bfloat16)
    kernel_grad = jnp.stack([transposed_times(shifted[tap_index], inner_grad) for tap_index in range(3)])
    return (kernel_grad, mixing_grad, inner_grad)

def window_gradients(window_rows, window_layout, window_length, window_targets, projection, kernels, mixers, readout):
    row_ids = jnp.arange(ROWS_DEV, dtype=jnp.int32)
    owner_shard = row_ids // BLOCK
    slot_ids = jnp.take(window_layout, owner_shard, axis=1)
    position = owner_shard[None, :] * ROWS_DEV + slot_ids * BLOCK + (row_ids % BLOCK)[None, :]
    position = position.reshape(N_SEQ * ROWS_DEV).astype(jnp.int32)
    inside = (position < window_length).astype(jnp.float32)
    projected = (matmul(window_rows.reshape(N_SEQ * ROWS_DEV, EMB), projection) * inside[:, None]).astype(jnp.bfloat16)
    hidden = jnp.zeros((POSITIONS, CH), jnp.bfloat16).at[position].set(projected)
    fine_active = gelu_exact(hidden.astype(jnp.float32)).astype(jnp.bfloat16)
    fine_shifted = padded_taps(fine_active, SPREAD_FINE)
    first_pooled, fine_inner, fine_gated = block_rest(hidden, fine_shifted, kernels[0], mixers[0])
    coarse_active = gelu_exact(first_pooled.astype(jnp.float32)).astype(jnp.bfloat16)
    coarse_shifted = padded_taps(coarse_active, SPREAD_COARSE)
    second, coarse_inner, coarse_gated = block_rest(first_pooled, coarse_shifted, kernels[1], mixers[1])
    logits = matmul(second, readout)
    bin_ids = jnp.arange(BINS, dtype=jnp.int32)
    valid_bins = (bin_ids * 4 < window_length).astype(jnp.float32)
    loss_scale = 2.0 / math.sqrt(WINDOWS * BINS)
    target_values = window_targets.astype(jnp.float32)
    logit_grad = (loss_scale * valid_bins[:, None] * (jax.nn.softplus(logits) - target_values) * jax.nn.sigmoid(logits)).astype(jnp.bfloat16)
    readout_grad = transposed_times(second, logit_grad)
    upper_grad = (times_transposed(logit_grad, readout) * 0.5).astype(jnp.bfloat16)
    upper_rows = jnp.repeat(upper_grad, 2, axis=0)
    coarse_kernel, coarse_mixing, coarse_grad = block_backward(upper_rows, coarse_shifted, coarse_inner, coarse_gated, kernels[1], mixers[1])
    half_count = coarse_grad.shape[0]
    grad_wide = jnp.pad(coarse_grad, ((SPREAD_COARSE, SPREAD_COARSE), (0, 0)))
    input_grad = times_transposed(grad_wide[2 * SPREAD_COARSE:2 * SPREAD_COARSE + half_count], kernels[1][0]) + times_transposed(coarse_grad, kernels[1][1]) + times_transposed(grad_wide[0:half_count], kernels[1][2])
    first_grad = upper_rows.astype(jnp.float32) + input_grad * gelu_slope(first_pooled.astype(jnp.float32))
    trunk_grad = first_grad * (math.sqrt(WINDOWS * BINS) * 0.5)
    lower_grad = (first_grad * 0.5).astype(jnp.bfloat16)
    lower_rows = jnp.repeat(lower_grad, 2, axis=0)
    fine_kernel, fine_mixing, fine_grad = block_backward(lower_rows, fine_shifted, fine_inner, fine_gated, kernels[0], mixers[0])
    return (jnp.stack([fine_kernel, coarse_kernel]), jnp.stack([fine_mixing, coarse_mixing]), readout_grad, trunk_grad)

def reference(embeddings, layout, lengths, targets, projection, kernels, mixers, readout):

    def one_window(inputs):
        return window_gradients(inputs[0], inputs[1], inputs[2], inputs[3], projection, kernels, mixers, readout)
    stacked = lax.map(one_window, (embeddings, layout, lengths, targets))
    return (lax.optimization_barrier(jnp.sum(stacked[0], axis=0)), lax.optimization_barrier(jnp.sum(stacked[1], axis=0)), lax.optimization_barrier(jnp.sum(stacked[2], axis=0)), stacked[3])
```

```python
import math

import jax
import jax.numpy as jnp
from jax import lax
from jax.experimental import pallas as pl
from jax.experimental.pallas import tpu as pltpu
from jax.sharding import PartitionSpec as P

SPREAD_FINE = 256
SPREAD_COARSE = 128
MESH = pl.DeviceIdType.MESH
CHUNK = 512
ORDERS = ((0, 1, 2), (1, 2, 0), (2, 0, 1))
WIDTHS = (384, 384, 512)


def place():
    dp, seq = lax.axis_index("dp"), lax.axis_index("seq")
    core = lax.rem(dp, 2)
    x = lax.rem(lax.div(seq, 4), 2) * 2 + lax.div(dp, 2)
    return (x, lax.div(seq, 8), lax.rem(seq, 4)), core


def device_at(coords, core):
    x, y, z = coords
    return (lax.rem(x, 2) * 2 + core, y * 8 + lax.div(x, 2) * 4 + z)


def moved(coords, axis, step):
    out = list(coords)
    out[axis] = lax.rem(out[axis] + step, 4)
    return tuple(out)


class Sender:
    def __init__(self, send_sems, recv_sems):
        self.send_sems, self.recv_sems, self.copies = send_sems, recv_sems, []

    def __call__(self, src, dst, device):
        at = len(self.copies)
        copy = pltpu.make_async_remote_copy(
            src_ref=src,
            dst_ref=dst,
            send_sem=self.send_sems.at[at],
            recv_sem=self.recv_sems.at[at],
            device_id=device,
            device_id_type=MESH,
        )
        copy.start()
        self.copies.append(copy)
        return copy

    def finish(self):
        for copy in self.copies:
            copy.wait_send()


def greet(devices):
    barrier = pltpu.get_barrier_semaphore()
    for device in devices:
        pl.semaphore_signal(barrier, inc=1, device_id=device, device_id_type=MESH)
    pl.semaphore_wait(barrier, len(devices))


def f32(values):
    return values.astype(jnp.float32)


def project_kernel(emb, weights, out, emb_v, w_v, acc, rows_v, landed, local_sems, send_sems, recv_sems, a2a_send, a2a_recv):
    coords, core = place()
    dp, seq = lax.axis_index("dp"), lax.axis_index("seq")
    groups = lax.axis_size("seq")
    depth = weights.shape[0]
    partner = device_at(coords, 1 - core)
    up, down = device_at(moved(coords, 0, 1), core), device_at(moved(coords, 0, 3), core)
    across = lax.rem(dp + 2, 4)
    order = (dp, dp + 1 - 2 * core, across, across + 1 - 2 * core)
    own_w = pltpu.make_async_copy(weights, w_v.at[dp], local_sems.at[4])
    own_w.start()
    loads = []
    for at, quarter in enumerate(order):
        cols = pl.ds(pl.multiple_of(quarter * depth, depth), depth)
        load = pltpu.make_async_copy(emb.at[:, cols], emb_v.at[:, cols], local_sems.at[at])
        load.start()
        loads.append(load)

    barrier = pltpu.get_barrier_semaphore()

    @pl.loop(1, groups)
    def _(off):
        pl.semaphore_signal(
            barrier, inc=1, device_id=(dp, lax.rem(seq + off, groups)), device_id_type=MESH
        )

    for device in (partner, up, down):
        pl.semaphore_signal(barrier, inc=1, device_id=device, device_id_type=MESH)
    pl.semaphore_wait(barrier, groups + 2)

    send = Sender(send_sems, recv_sems)
    crossing = []
    for part in range(2):
        for side, device in enumerate((up, down)):
            rows = pl.ds(side * (depth // 2) + part * CHUNK, CHUNK)
            crossing.append(send(weights.at[rows], w_v.at[dp, rows], device))
    to_partner = send(weights, w_v.at[dp], partner)

    def accumulate(quarter, row):
        cols = pl.ds(pl.multiple_of(quarter * depth + row, CHUNK), CHUNK)
        acc[...] += jnp.dot(
            emb_v[:, cols],
            w_v[quarter, pl.ds(pl.multiple_of(row, CHUNK), CHUNK), :],
            preferred_element_type=jnp.float32,
        )

    acc[...] = jnp.zeros_like(acc)
    loads[0].wait()
    own_w.wait()

    @pl.loop(0, depth // CHUNK)
    def _(step):
        accumulate(order[0], step * CHUNK)

    loads[1].wait()
    to_partner.wait_recv()

    @pl.loop(0, depth // CHUNK)
    def _(step):
        accumulate(order[1], step * CHUNK)

    loads[2].wait()
    loads[3].wait()
    relays = []
    for at, copy in enumerate(crossing):
        copy.wait_recv()
        row = (at % 2) * (depth // 2) + (at // 2) * CHUNK
        block = w_v.at[across, pl.ds(row, CHUNK)]
        relays.append(send(block, block, partner))
        accumulate(across, row)
    for at, copy in enumerate(relays):
        copy.wait_recv()
        accumulate(order[3], (at % 2) * (depth // 2) + (at // 2) * CHUNK)

    block_rows = rows_v.shape[1]
    rows_v[...] = acc[...].astype(jnp.bfloat16).reshape(rows_v.shape)

    def block_copy(off):
        there = lax.rem(seq + off, groups)
        return pltpu.make_async_remote_copy(
            src_ref=rows_v.at[there],
            dst_ref=landed.at[seq],
            send_sem=a2a_send.at[off],
            recv_sem=a2a_recv.at[off],
            device_id=(dp, there),
            device_id_type=MESH,
        )

    @pl.loop(1, groups)
    def _(off):
        block_copy(off).start()

    landed[seq] = rows_v[seq]

    @pl.loop(1, groups)
    def _(off):
        block_copy(off).wait()

    send.finish()
    out[...] = landed[...]


def project_and_exchange(emb, weights):
    rows, emb_width = emb.shape
    depth, channels = weights.shape
    groups = lax.axis_size("seq")
    blocks = (groups, rows // groups, channels)
    n_copies = 9
    return pl.pallas_call(
        project_kernel,
        out_shape=jax.ShapeDtypeStruct(blocks, jnp.bfloat16),
        in_specs=[pl.BlockSpec(memory_space=pl.ANY)] * 2,
        out_specs=pl.BlockSpec(memory_space=pltpu.VMEM),
        scratch_shapes=[
            pltpu.VMEM((rows, emb_width), jnp.bfloat16),
            pltpu.VMEM((4, depth, channels), jnp.bfloat16),
            pltpu.VMEM((rows, channels), jnp.float32),
            pltpu.VMEM(blocks, jnp.bfloat16),
            pltpu.VMEM(blocks, jnp.bfloat16),
            pltpu.SemaphoreType.DMA((5,)),
            pltpu.SemaphoreType.DMA((n_copies,)),
            pltpu.SemaphoreType.DMA((n_copies,)),
            pltpu.SemaphoreType.DMA((groups,)),
            pltpu.SemaphoreType.DMA((groups,)),
        ],
        compiler_params=pltpu.CompilerParams(
            collective_id=0, has_side_effects=True, vmem_limit_bytes=56 << 20
        ),
        name="project",
    )(emb, weights)


class Part:
    def __init__(self, order, terms, scratch, send, coords, core):
        self.order, self.terms, self.send, self.coords, self.core = order, terms, send, coords, core
        (self.pair, self.acc1, self.halves1, self.acc2, self.halves2, self.acc3, self.last) = scratch

    def start_pair(self):
        self.pair_copy = self.send(
            self.terms.at[1 - self.core], self.pair, device_at(self.coords, 1 - self.core)
        )

    def end_pair(self):
        self.pair_copy.wait_recv()

        @pl.loop(0, 4)
        def _(at):
            self.acc1[at] = (f32(self.terms[self.core, at]) + f32(self.pair[at])).astype(jnp.bfloat16)

    def level(self, number):
        acc, halves = (self.acc1, self.halves1) if number == 0 else (self.acc2, self.halves2)
        axis = self.order[number]
        here = self.coords[axis]
        up, down = (device_at(moved(self.coords, axis, k), self.core) for k in (1, 3))
        return acc, halves, here, up, down

    def start_level(self, number):
        acc, halves, here, up, down = self.level(number)
        after, before, opposite = (lax.rem(here + k, 4) for k in (1, 3, 2))
        low, high = pl.ds(0, 2), pl.ds(2, 2)
        self.arrivals = [
            self.send(acc.at[opposite, low], halves.at[0], up),
            self.send(acc.at[opposite, high], halves.at[1], down),
            self.send(acc.at[before, low], halves.at[2], down),
            self.send(acc.at[after, high], halves.at[3], up),
        ]

    def relay_level(self, number):
        acc, halves, here, up, down = self.level(number)
        after, before = (lax.rem(here + k, 4) for k in (1, 3))
        self.arrivals[0].wait_recv()
        halves[4] = (f32(halves[0]) + f32(acc[after, 0:2])).astype(jnp.bfloat16)
        self.arrivals.append(self.send(halves.at[4], halves.at[6], up))
        self.arrivals[1].wait_recv()
        halves[5] = (f32(halves[1]) + f32(acc[before, 2:4])).astype(jnp.bfloat16)
        self.arrivals.append(self.send(halves.at[5], halves.at[7], down))

    def end_level(self, number):
        acc, halves, here, _, _ = self.level(number)
        into = self.acc2 if number == 0 else self.acc3
        for copy in self.arrivals[2:]:
            copy.wait_recv()
        into[0:2] = (f32(acc[here, 0:2]) + f32(halves[2]) + f32(halves[6])).astype(jnp.bfloat16)
        into[2:4] = (f32(acc[here, 2:4]) + f32(halves[3]) + f32(halves[7])).astype(jnp.bfloat16)

    def start_last(self):
        axis = self.order[2]
        here = self.coords[axis]
        self.arrivals = [
            self.send(
                self.acc3.at[lax.rem(here + k, 4)],
                self.last.at[k - 1],
                device_at(moved(self.coords, axis, k), self.core),
            )
            for k in (1, 2, 3)
        ]

    def end_last(self):
        here = self.coords[self.order[2]]
        for copy in self.arrivals:
            copy.wait_recv()
        return f32(self.acc3[here]) + f32(self.last[0]) + f32(self.last[1]) + f32(self.last[2])


N_REDUCE = 3 * (1 + 6 + 6 + 3) + 3


def reduce_kernel(terms0, terms1, terms2, kernel_out, mixer_out, readout_out, *scratch):
    parts_scratch, (joined, send_sems, recv_sems) = scratch[:-3], scratch[-3:]
    coords, core = place()
    dp = lax.axis_index("dp")
    send = Sender(send_sems, recv_sems)
    parts = [
        Part(ORDERS[at], terms, parts_scratch[7 * at : 7 * at + 7], send, coords, core)
        for at, terms in enumerate((terms0, terms1, terms2))
    ]
    pair_x = (coords[0] + 1 - 2 * lax.rem(coords[0], 2),) + coords[1:]
    partner = device_at(coords, 1 - core)
    group = [partner, device_at(pair_x, core), device_at(pair_x, 1 - core)]
    greet(
        [device_at(moved(coords, axis, k), core) for axis in range(3) for k in (1, 2, 3)]
        + [partner, device_at(pair_x, 1 - core)]
    )
    for part in parts:
        part.start_pair()
    for part in parts:
        part.end_pair()
        part.start_level(0)
    for part in parts:
        part.relay_level(0)
    for part in parts:
        part.end_level(0)
        part.start_level(1)
    for part in parts:
        part.relay_level(1)
    for part in parts:
        part.end_level(1)
        part.start_last()
    joined[dp, :, 0:384] = parts[0].end_last()
    joined[dp, :, 384:768] = parts[1].end_last()
    mine = joined.at[dp]
    last = [send(mine, mine, device) for device in group]
    readout_out[...] = parts[2].end_last()
    for copy in last:
        copy.wait_recv()
    for index in range(4):

        @pl.when(dp == index)
        def _():
            low = 96 * index
            for tap in range(6):
                slot, start = (tap, low) if tap < 4 else (tap - 4, 384 + low)
                kernel_out[tap] = joined[slot, :, start : start + 96]
            slot, start = 2 + index // 2, 384 + 192 * (index % 2)
            mixer_out[0] = joined[slot, 0:12, start : start + 192]
            mixer_out[1] = joined[slot, 12:24, start : start + 192]

    send.finish()


def part_scratch(width):
    unit = (24, width)
    return [
        pltpu.VMEM(shape + unit, jnp.bfloat16)
        for shape in ((4, 4, 4), (4, 4, 4), (8, 2, 4), (4, 4), (8, 2), (4,), (3,))
    ]


def reduce_terms(terms):
    vmem = pl.BlockSpec(memory_space=pltpu.VMEM)
    return pl.pallas_call(
        reduce_kernel,
        out_shape=(
            jax.ShapeDtypeStruct((6, 24, 96), jnp.float32),
            jax.ShapeDtypeStruct((2, 12, 192), jnp.float32),
            jax.ShapeDtypeStruct((24, 512), jnp.float32),
        ),
        in_specs=[vmem] * 3,
        out_specs=[vmem] * 3,
        scratch_shapes=[s for width in WIDTHS for s in part_scratch(width)]
        + [
            pltpu.VMEM((4, 24, 768), jnp.float32),
            pltpu.SemaphoreType.DMA((N_REDUCE,)),
            pltpu.SemaphoreType.DMA((N_REDUCE,)),
        ],
        compiler_params=pltpu.CompilerParams(
            collective_id=2, has_side_effects=True, vmem_limit_bytes=56 << 20
        ),
        name="reduce_gradients",
    )(*terms)


def arrange_terms(kernel_terms, mixer_terms, readout_terms):
    bf16 = jnp.bfloat16
    kernels = kernel_terms.astype(bf16).reshape(6, 768, 384)
    mixers = mixer_terms.astype(bf16).reshape(2, 32, 12, 768).transpose(1, 0, 2, 3).reshape(768, 2, 384)
    first = kernels[:4].reshape(2, 2, 4, 2, 4, 24, 384)
    second = jnp.concatenate([kernels[4:], mixers.transpose(1, 0, 2)]).reshape(2, 2, 4, 2, 4, 24, 384)
    third = readout_terms.astype(bf16).reshape(4, 2, 4, 24, 2, 2, 512).transpose(4, 5, 0, 1, 2, 3, 6)
    return (
        first.transpose(1, 3, 0, 2, 4, 5, 6).reshape(2, 4, 4, 4, 24, 384),
        second.transpose(1, 2, 4, 3, 0, 5, 6).reshape(2, 4, 4, 4, 24, 384),
        third.transpose(1, 4, 3, 0, 2, 5, 6).reshape(2, 4, 4, 4, 24, 512),
    )


def with_halo(shard, sides, width):
    for axis, dim in sides:
        size, length = (lax.axis_size(axis), shard.shape[dim])
        up = [(i, (i + 1) % size) for i in range(size - 1)]
        down = [(j, i) for i, j in up]
        last = lax.slice_in_dim(shard, length - width, length, axis=dim)
        leading = lax.slice_in_dim(shard, 0, width, axis=dim)
        before = lax.ppermute(last, axis, up)
        after = lax.ppermute(leading, axis, down)
        shard = jnp.concatenate([before, shard, after], axis=dim)
    return shard


def gelu_exact(values):
    return 0.5 * values * (1.0 + lax.erf(values * (1.0 / math.sqrt(2.0))))


def gelu_slope(values):
    cumulative = 0.5 * (1.0 + lax.erf(values * (1.0 / math.sqrt(2.0))))
    density = jnp.exp(-0.5 * values * values) * (1.0 / math.sqrt(2.0 * math.pi))
    return cumulative + values * density


def matmul(left_side, right_side):
    return jnp.dot(left_side, right_side, preferred_element_type=jnp.float32)


def times_transposed(left_side, right_side):
    return lax.dot_general(
        left_side, right_side, (((1,), (1,)), ((), ())), preferred_element_type=jnp.float32
    )


def transposed_times(left_side, right_side):
    return lax.dot_general(
        left_side, right_side, (((0,), (0,)), ((), ())), preferred_element_type=jnp.float32
    )


def spread_taps(extended, spread, row_count):
    return (
        extended[0:row_count],
        extended[spread : spread + row_count],
        extended[2 * spread : 2 * spread + row_count],
    )


def block_rest(hidden, shifted, kernel, mixing):
    inner_sum = (
        matmul(shifted[0], kernel[0])
        + matmul(shifted[1], kernel[1])
        + matmul(shifted[2], kernel[2])
    )
    gated_out = gelu_exact(inner_sum).astype(jnp.bfloat16)
    output = hidden.astype(jnp.float32) + matmul(gated_out, mixing)
    pooled = (output.reshape(-1, 2, output.shape[1]).sum(axis=1) * 0.5).astype(jnp.bfloat16)
    return (pooled, inner_sum, gated_out)


def block_backward(upstream, shifted, inner_sum, gated_out, mixing):
    mixing_grad = transposed_times(gated_out, upstream)
    inner_grad = (times_transposed(upstream, mixing) * gelu_slope(inner_sum)).astype(jnp.bfloat16)
    kernel_grad = jnp.stack(
        [transposed_times(shifted[tap_index], inner_grad) for tap_index in range(3)]
    )
    return (kernel_grad, mixing_grad, inner_grad)


def shards(embeddings, layout, lengths, targets, projection, kernels, mixers, readout):
    groups = lax.axis_size("seq")
    windows_total = lax.axis_size("dp")
    device = lax.axis_index("seq")
    local_rows = embeddings[0, 0]
    row_count = local_rows.shape[0]
    block_rows = row_count // groups
    channels = projection.shape[1]
    layout_table = layout[0]
    length = lengths[0]
    shard_ids = jnp.arange(groups, dtype=jnp.int32)
    own_column = lax.dynamic_index_in_dim(layout_table, device, axis=1, keepdims=False)
    matches = (own_column[:, None] == shard_ids[None, :]).astype(jnp.int32)
    source_index = jnp.sum(shard_ids[:, None] * matches, axis=0)
    received = project_and_exchange(local_rows, projection)
    hidden = jnp.take(received, source_index, axis=0).reshape(row_count, channels)
    positions = device * row_count + jnp.arange(row_count, dtype=jnp.int32)
    hidden = jnp.where((positions < length)[:, None], hidden, jnp.zeros_like(hidden))
    fine_spread = SPREAD_FINE
    coarse_spread = SPREAD_COARSE
    half_count = row_count // 2
    fine_active = gelu_exact(hidden.astype(jnp.float32)).astype(jnp.bfloat16)
    fine_wide = with_halo(fine_active, (("seq", 0),), fine_spread)
    fine_shifted = spread_taps(fine_wide, fine_spread, row_count)
    first_pooled, fine_inner, fine_gated = block_rest(hidden, fine_shifted, kernels[0], mixers[0])
    coarse_active = gelu_exact(first_pooled.astype(jnp.float32)).astype(jnp.bfloat16)
    coarse_wide = with_halo(coarse_active, (("seq", 0),), coarse_spread)
    coarse_shifted = spread_taps(coarse_wide, coarse_spread, half_count)
    second, coarse_inner, coarse_gated = block_rest(
        first_pooled, coarse_shifted, kernels[1], mixers[1]
    )
    bin_count = row_count // 4
    logits = matmul(second, readout)
    bin_ids = device * bin_count + jnp.arange(bin_count, dtype=jnp.int32)
    valid_bins = (bin_ids * 4 < length).astype(jnp.float32)
    loss_scale = 2.0 / math.sqrt(windows_total * groups * bin_count)
    target_values = targets[0].astype(jnp.float32)
    logit_grad = (
        loss_scale
        * valid_bins[:, None]
        * (jax.nn.softplus(logits) - target_values)
        * jax.nn.sigmoid(logits)
    ).astype(jnp.bfloat16)
    readout_grad = transposed_times(second, logit_grad)
    upper_grad = (times_transposed(logit_grad, readout) * 0.5).astype(jnp.bfloat16)
    upper_rows = jnp.repeat(upper_grad, 2, axis=0)
    coarse_kernel, coarse_mixing, coarse_grad = block_backward(
        upper_rows, coarse_shifted, coarse_inner, coarse_gated, mixers[1]
    )
    grad_wide = with_halo(coarse_grad, (("seq", 0),), coarse_spread)
    input_grad = (
        times_transposed(
            grad_wide[2 * coarse_spread : 2 * coarse_spread + half_count], kernels[1][0]
        )
        + times_transposed(coarse_grad, kernels[1][1])
        + times_transposed(grad_wide[0:half_count], kernels[1][2])
    )
    first_grad = upper_rows.astype(jnp.float32) + input_grad * gelu_slope(
        first_pooled.astype(jnp.float32)
    )
    trunk_grad = first_grad * (math.sqrt(windows_total * groups * bin_count) * 0.5)
    lower_grad = (first_grad * 0.5).astype(jnp.bfloat16)
    lower_rows = jnp.repeat(lower_grad, 2, axis=0)
    fine_kernel, fine_mixing, fine_grad = block_backward(
        lower_rows, fine_shifted, fine_inner, fine_gated, mixers[0]
    )
    kernel_terms = jnp.stack([fine_kernel, coarse_kernel])
    mixer_terms = jnp.stack([fine_mixing, coarse_mixing])
    kernel_total, mixer_total, readout_total = reduce_terms(
        arrange_terms(kernel_terms, mixer_terms, readout_grad)
    )
    return (kernel_total.reshape(2, 3, 24, 96), mixer_total, readout_total, trunk_grad[None])


def solution(mesh):
    placed = (
        P("dp", "seq", None, None),
        P("dp", None, None),
        P("dp"),
        P("dp", "seq", None),
        P("dp", None),
        P(),
        P(),
        P(),
    )
    return jax.shard_map(
        shards,
        mesh=mesh,
        in_specs=placed,
        out_specs=(
            P(None, None, "seq", "dp"),
            P(None, "seq", "dp"),
            P("seq", "dp"),
            P("dp", "seq", None),
        ),
        check_vma=False,
    )
```

```python
import math

import jax
import jax.numpy as jnp
from jax import lax
from jax.experimental import pallas as pl
from jax.experimental.pallas import tpu as pltpu
from jax.sharding import PartitionSpec as P

MESH = pl.DeviceIdType.MESH
CHUNK = 512
ORDERS = ((0, 1, 2), (1, 2, 0), (2, 0, 1))
WIDTHS = (384, 384, 512)


def place():
    dp, seq = lax.axis_index("dp"), lax.axis_index("seq")
    core = lax.rem(dp, 2)
    x = lax.rem(lax.div(seq, 4), 2) * 2 + lax.div(dp, 2)
    return (x, lax.div(seq, 8), lax.rem(seq, 4)), core


def device_at(coords, core):
    x, y, z = coords
    return (lax.rem(x, 2) * 2 + core, y * 8 + lax.div(x, 2) * 4 + z)


def moved(coords, axis, step):
    out = list(coords)
    out[axis] = lax.rem(out[axis] + step, 4)
    return tuple(out)


class Sender:
    def __init__(self, send_sems, recv_sems):
        self.send_sems, self.recv_sems, self.copies = send_sems, recv_sems, []

    def __call__(self, src, dst, device):
        at = len(self.copies)
        copy = pltpu.make_async_remote_copy(
            src_ref=src,
            dst_ref=dst,
            send_sem=self.send_sems.at[at],
            recv_sem=self.recv_sems.at[at],
            device_id=device,
            device_id_type=MESH,
        )
        copy.start()
        self.copies.append(copy)
        return copy

    def finish(self):
        for copy in self.copies:
            copy.wait_send()


def greet(devices):
    barrier = pltpu.get_barrier_semaphore()
    for device in devices:
        pl.semaphore_signal(barrier, inc=1, device_id=device, device_id_type=MESH)
    pl.semaphore_wait(barrier, len(devices))


def f32(values):
    return values.astype(jnp.float32)


def project_kernel(emb, weights, out, emb_v, w_v, acc, rows_v, landed, local_sems, send_sems, recv_sems, a2a_send, a2a_recv):
    coords, core = place()
    dp, seq = lax.axis_index("dp"), lax.axis_index("seq")
    groups = lax.axis_size("seq")
    depth = weights.shape[0]
    partner = device_at(coords, 1 - core)
    up, down = device_at(moved(coords, 0, 1), core), device_at(moved(coords, 0, 3), core)
    across = lax.rem(dp + 2, 4)
    order = (dp, dp + 1 - 2 * core, across, across + 1 - 2 * core)
    own_w = pltpu.make_async_copy(weights, w_v.at[dp], local_sems.at[4])
    own_w.start()
    loads = []
    for at, quarter in enumerate(order):
        cols = pl.ds(pl.multiple_of(quarter * depth, depth), depth)
        load = pltpu.make_async_copy(emb.at[:, cols], emb_v.at[:, cols], local_sems.at[at])
        load.start()
        loads.append(load)

    barrier = pltpu.get_barrier_semaphore()

    @pl.loop(1, groups)
    def _(off):
        pl.semaphore_signal(
            barrier, inc=1, device_id=(dp, lax.rem(seq + off, groups)), device_id_type=MESH
        )

    for device in (partner, up, down):
        pl.semaphore_signal(barrier, inc=1, device_id=device, device_id_type=MESH)
    pl.semaphore_wait(barrier, groups + 2)

    send = Sender(send_sems, recv_sems)
    crossing = []
    for part in range(2):
        for side, device in enumerate((up, down)):
            rows = pl.ds(side * (depth // 2) + part * CHUNK, CHUNK)
            crossing.append(send(weights.at[rows], w_v.at[dp, rows], device))
    to_partner = send(weights, w_v.at[dp], partner)

    def accumulate(quarter, row):
        cols = pl.ds(pl.multiple_of(quarter * depth + row, CHUNK), CHUNK)
        acc[...] += jnp.dot(
            emb_v[:, cols],
            w_v[quarter, pl.ds(pl.multiple_of(row, CHUNK), CHUNK), :],
            preferred_element_type=jnp.float32,
        )

    acc[...] = jnp.zeros_like(acc)
    loads[0].wait()
    own_w.wait()

    @pl.loop(0, depth // CHUNK)
    def _(step):
        accumulate(order[0], step * CHUNK)

    loads[1].wait()
    to_partner.wait_recv()

    @pl.loop(0, depth // CHUNK)
    def _(step):
        accumulate(order[1], step * CHUNK)

    loads[2].wait()
    loads[3].wait()
    relays = []
    for at, copy in enumerate(crossing):
        copy.wait_recv()
        row = (at % 2) * (depth // 2) + (at // 2) * CHUNK
        block = w_v.at[across, pl.ds(row, CHUNK)]
        relays.append(send(block, block, partner))
        accumulate(across, row)
    for at, copy in enumerate(relays):
        copy.wait_recv()
        accumulate(order[3], (at % 2) * (depth // 2) + (at // 2) * CHUNK)

    block_rows = rows_v.shape[1]
    rows_v[...] = acc[...].astype(jnp.bfloat16).reshape(rows_v.shape)

    def block_copy(off):
        there = lax.rem(seq + off, groups)
        return pltpu.make_async_remote_copy(
            src_ref=rows_v.at[there],
            dst_ref=landed.at[seq],
            send_sem=a2a_send.at[off],
            recv_sem=a2a_recv.at[off],
            device_id=(dp, there),
            device_id_type=MESH,
        )

    @pl.loop(1, groups)
    def _(off):
        block_copy(off).start()

    landed[seq] = rows_v[seq]

    @pl.loop(1, groups)
    def _(off):
        block_copy(off).wait()

    send.finish()
    out[...] = landed[...]


def project_and_exchange(emb, weights):
    rows, emb_width = emb.shape
    depth, channels = weights.shape
    groups = lax.axis_size("seq")
    blocks = (groups, rows // groups, channels)
    n_copies = 9
    return pl.pallas_call(
        project_kernel,
        out_shape=jax.ShapeDtypeStruct(blocks, jnp.bfloat16),
        in_specs=[pl.BlockSpec(memory_space=pl.ANY)] * 2,
        out_specs=pl.BlockSpec(memory_space=pltpu.VMEM),
        scratch_shapes=[
            pltpu.VMEM((rows, emb_width), jnp.bfloat16),
            pltpu.VMEM((4, depth, channels), jnp.bfloat16),
            pltpu.VMEM((rows, channels), jnp.float32),
            pltpu.VMEM(blocks, jnp.bfloat16),
            pltpu.VMEM(blocks, jnp.bfloat16),
            pltpu.SemaphoreType.DMA((5,)),
            pltpu.SemaphoreType.DMA((n_copies,)),
            pltpu.SemaphoreType.DMA((n_copies,)),
            pltpu.SemaphoreType.DMA((groups,)),
            pltpu.SemaphoreType.DMA((groups,)),
        ],
        compiler_params=pltpu.CompilerParams(
            collective_id=0, has_side_effects=True, vmem_limit_bytes=56 << 20
        ),
        name="project",
    )(emb, weights)


class Part:
    def __init__(self, order, terms, scratch, send, coords, core):
        self.order, self.terms, self.send, self.coords, self.core = order, terms, send, coords, core
        (self.pair, self.acc1, self.halves1, self.acc2, self.halves2, self.acc3, self.last) = scratch

    def start_pair(self):
        self.pair_copy = self.send(
            self.terms.at[1 - self.core], self.pair, device_at(self.coords, 1 - self.core)
        )

    def end_pair(self):
        self.pair_copy.wait_recv()

        @pl.loop(0, 4)
        def _(at):
            self.acc1[at] = (f32(self.terms[self.core, at]) + f32(self.pair[at])).astype(jnp.bfloat16)

    def level(self, number):
        acc, halves = (self.acc1, self.halves1) if number == 0 else (self.acc2, self.halves2)
        axis = self.order[number]
        here = self.coords[axis]
        up, down = (device_at(moved(self.coords, axis, k), self.core) for k in (1, 3))
        return acc, halves, here, up, down

    def start_level(self, number):
        acc, halves, here, up, down = self.level(number)
        after, before, opposite = (lax.rem(here + k, 4) for k in (1, 3, 2))
        low, high = pl.ds(0, 2), pl.ds(2, 2)
        self.arrivals = [
            self.send(acc.at[opposite, low], halves.at[0], up),
            self.send(acc.at[opposite, high], halves.at[1], down),
            self.send(acc.at[before, low], halves.at[2], down),
            self.send(acc.at[after, high], halves.at[3], up),
        ]

    def relay_level(self, number):
        acc, halves, here, up, down = self.level(number)
        after, before = (lax.rem(here + k, 4) for k in (1, 3))
        self.arrivals[0].wait_recv()
        halves[4] = (f32(halves[0]) + f32(acc[after, 0:2])).astype(jnp.bfloat16)
        self.arrivals.append(self.send(halves.at[4], halves.at[6], up))
        self.arrivals[1].wait_recv()
        halves[5] = (f32(halves[1]) + f32(acc[before, 2:4])).astype(jnp.bfloat16)
        self.arrivals.append(self.send(halves.at[5], halves.at[7], down))

    def end_level(self, number):
        acc, halves, here, _, _ = self.level(number)
        into = self.acc2 if number == 0 else self.acc3
        for copy in self.arrivals[2:]:
            copy.wait_recv()
        into[0:2] = (f32(acc[here, 0:2]) + f32(halves[2]) + f32(halves[6])).astype(jnp.bfloat16)
        into[2:4] = (f32(acc[here, 2:4]) + f32(halves[3]) + f32(halves[7])).astype(jnp.bfloat16)

    def start_last(self):
        axis = self.order[2]
        here = self.coords[axis]
        self.arrivals = [
            self.send(
                self.acc3.at[lax.rem(here + k, 4)],
                self.last.at[k - 1],
                device_at(moved(self.coords, axis, k), self.core),
            )
            for k in (1, 2, 3)
        ]

    def end_last(self):
        here = self.coords[self.order[2]]
        for copy in self.arrivals:
            copy.wait_recv()
        return f32(self.acc3[here]) + f32(self.last[0]) + f32(self.last[1]) + f32(self.last[2])


def part_scratch(width):
    unit = (24, width)
    return [
        pltpu.VMEM(shape + unit, jnp.bfloat16)
        for shape in ((4, 4, 4), (4, 4, 4), (8, 2, 4), (4, 4), (8, 2), (4,), (3,))
    ]


def gelu(values):
    return 0.5 * values * (1.0 + lax.erf(values * (1.0 / math.sqrt(2.0))))


def gelu_slope(values):
    cumulative = 0.5 * (1.0 + lax.erf(values * (1.0 / math.sqrt(2.0))))
    density = jnp.exp(-0.5 * values * values) * (1.0 / math.sqrt(2.0 * math.pi))
    return cumulative + values * density


def bf(values):
    return values.astype(jnp.bfloat16)


def dot(left, right):
    return jnp.dot(left, right, preferred_element_type=jnp.float32)


def dot_nt(left, right):
    return lax.dot_general(
        left, right, (((1,), (1,)), ((), ())), preferred_element_type=jnp.float32
    )


def flat(values):
    return values.reshape(-1, values.shape[-1])


def row_blocks(count, step, body):
    @pl.loop(0, count // step)
    def _(at):
        body(pl.multiple_of(at * step, step))


STEP = 16
HALF = 64
INNER = 384
CH = 768


def conv_forward(act, kernel, inner, edge_out, edge_in, send, after, before, seq, groups):
    low, high = flat(act[:, 0:HALF, :]), flat(act[:, HALF:128, :])
    shape = (act.shape[0], HALF, INNER)
    edge_out[0] = bf(dot(high, kernel[0])).reshape(shape)
    from_before = send(edge_out.at[0], edge_in.at[0], after)
    edge_out[1] = bf(dot(low, kernel[2])).reshape(shape)
    from_after = send(edge_out.at[1], edge_in.at[1], before)
    inner[:, 0:HALF, :] = (dot(low, kernel[1]) + dot(high, kernel[2])).reshape(shape)
    inner[:, HALF:128, :] = (dot(high, kernel[1]) + dot(low, kernel[0])).reshape(shape)
    return from_before, from_after


def finish_inner(inner, gated, edge_in, copies, seq, groups):
    copies[0].wait_recv()
    copies[1].wait_recv()
    keeps = (jnp.where(seq == 0, 0.0, 1.0), jnp.where(seq == groups - 1, 0.0, 1.0))
    for side in range(2):

        @pl.loop(0, inner.shape[0])
        def _(group):
            for row in range(0, HALF, STEP):
                rows = slice(side * HALF + row, side * HALF + row + STEP)
                total = inner[group, rows, :] + f32(edge_in[side, group, row : row + STEP, :]) * keeps[side]
                inner[group, rows, :] = total
                gated[group, rows, :] = bf(gelu(total))


def exchange_grads(wide, send, after, before):
    from_after = send(wide.at[1, :, pl.ds(0, HALF)], wide.at[0, :, pl.ds(HALF, HALF)], before)
    from_before = send(wide.at[1, :, pl.ds(HALF, HALF)], wide.at[2, :, pl.ds(0, HALF)], after)
    wide[0, :, 0:HALF, :] = wide[1, :, HALF:128, :]
    wide[2, :, HALF:128, :] = wide[1, :, 0:HALF, :]
    return from_after, from_before


def finish_exchange(wide, copies, seq, groups):
    copies[0].wait_recv()
    copies[1].wait_recv()
    zeros = jnp.zeros((wide.shape[1], HALF, INNER), jnp.bfloat16)

    @pl.when(seq == groups - 1)
    def _():
        wide[0, :, HALF:128, :] = zeros

    @pl.when(seq == 0)
    def _():
        wide[2, :, 0:HALF, :] = zeros


def gradient_rows(transposed, right, store):
    @pl.loop(0, 4)
    def _(y):
        result = dot(transposed[pl.ds(pl.multiple_of(y * 192, 64), 192), :], right())
        for x_hi in range(2):
            for z in range(4):
                row = 24 * (4 * x_hi + z)
                store(y, x_hi, z, bf(result[row : row + 24]))


def blocks_kernel(
    landed, lane_position, length_ref, targets, kernels, mixers, readout,
    kernel_out, mixer_out, readout_out, trunk_out,
    kernels_v, mixers_v, readout_v, targets_v, local_sems,
    hid, act1, inner1, gated1, mixed, first, act2, inner2, gated2, second, logits, logit_grad,
    upper, woven, wide2, wide1, lower, act1_t, act2_t, second_t, mixer_left, mixer_right,
    edge1_out, edge1_in, edge2_out, edge2_in, terms0, terms1, terms2, *rest
):
    parts_scratch, (joined, send_sems, recv_sems) = rest[:-3], rest[-3:]
    coords, core = place()
    dp, seq = lax.axis_index("dp"), lax.axis_index("seq")
    groups = lax.axis_size("seq")
    loads = []
    for at, (src, dst) in enumerate(
        (
            (kernels.at[0], kernels_v.at[0]),
            (mixers, mixers_v),
            (kernels.at[1], kernels_v.at[1]),
            (readout, readout_v),
            (targets, targets_v),
        )
    ):
        loads.append(pltpu.make_async_copy(src, dst, local_sems.at[at]))
        loads[-1].start()
    after, before = (dp, lax.rem(seq + 1, groups)), (dp, lax.rem(seq + groups - 1, groups))
    send = Sender(send_sems, recv_sems)
    all_terms = (terms0, terms1, terms2)
    parts = [
        Part(ORDERS[at], all_terms[at], parts_scratch[7 * at : 7 * at + 7], send, coords, core)
        for at in range(3)
    ]
    pair_x = (coords[0] + 1 - 2 * lax.rem(coords[0], 2),) + coords[1:]
    partner = device_at(coords, 1 - core)
    group = [partner, device_at(pair_x, core), device_at(pair_x, 1 - core)]
    greet(
        [device_at(moved(coords, axis, k), core) for axis in range(3) for k in (1, 2, 3)]
        + [partner, device_at(pair_x, 1 - core), after, before]
    )
    length = length_ref[0]

    blocks = flat(landed[...])
    for group_at in range(4):
        spot = 4 * lax.broadcasted_iota(jnp.int32, (128, 512), 0) + group_at
        chosen = (lane_position[...] == spot) & (spot + seq * 512 < length)
        hid[group_at] = bf(dot(jnp.where(chosen, 1.0, 0.0).astype(jnp.bfloat16), blocks))

    for group_at in range(4):

        def gelu_rows(row, group_at=group_at):
            act1[group_at, pl.ds(row, STEP), :] = bf(gelu(f32(hid[group_at, pl.ds(row, STEP), :])))

        row_blocks(128, STEP, gelu_rows)

    loads[0].wait()
    edges = conv_forward(act1, kernels_v.at[0], inner1, edge1_out, edge1_in, send, after, before, seq, groups)
    act1_t[...] = flat(act1[...]).T
    finish_inner(inner1, gated1, edge1_in, edges, seq, groups)
    loads[1].wait()
    mixed[...] = dot(flat(gated1[...]), mixers_v[0]).reshape(mixed.shape)
    for pair in range(2):

        def pool_rows(row, pair=pair):
            rows = pl.ds(row, STEP)
            total = (f32(hid[2 * pair, rows, :]) + mixed[2 * pair, rows, :]) + (
                f32(hid[2 * pair + 1, rows, :]) + mixed[2 * pair + 1, rows, :]
            )
            pooled = bf(total * 0.5)
            first[pair, rows, :] = pooled
            act2[pair, rows, :] = bf(gelu(f32(pooled)))

        row_blocks(128, STEP, pool_rows)

    loads[2].wait()
    edges = conv_forward(act2, kernels_v.at[1], inner2, edge2_out, edge2_in, send, after, before, seq, groups)
    act2_t[...] = flat(act2[...]).T
    finish_inner(inner2, gated2, edge2_in, edges, seq, groups)
    mixed[0:2] = dot(flat(gated2[...]), mixers_v[1]).reshape(2, 128, CH)

    def pool_again(row):
        rows = pl.ds(row, STEP)
        total = (f32(first[0, rows, :]) + mixed[0, rows, :]) + (f32(first[1, rows, :]) + mixed[1, rows, :])
        second[rows, :] = bf(total * 0.5)

    row_blocks(128, STEP, pool_again)
    loads[3].wait()
    loads[4].wait()
    logits[...] = dot(second[...], readout_v[...])
    loss_scale = 2.0 / math.sqrt(lax.axis_size("dp") * groups * 128)

    def loss_rows(row):
        rows = pl.ds(row, 8)
        values = logits[rows, :]
        small = jnp.exp(-jnp.abs(values))
        softplus = jnp.maximum(values, 0.0) + jnp.log1p(small)
        sigmoid = jnp.where(values >= 0.0, 1.0, small) / (1.0 + small)
        bins = seq * 128 + row + lax.broadcasted_iota(jnp.int32, (8, 1), 0)
        valid = jnp.where(bins * 4 < length, loss_scale, 0.0)
        mixed_rows = valid * (softplus - targets_v[rows, :].astype(jnp.float32)) * sigmoid
        logits[rows, :] = mixed_rows

    row_blocks(128, 8, loss_rows)
    logit_grad[...] = bf(logits[...])
    second_t[...] = second[...].T
    for index in range(4):
        x_lo, half = index // 2, index % 2

        def store(y, x_hi, z, block, x_lo=x_lo, half=half):
            terms2[half, z, 2 * x_hi + x_lo, y] = block

        gradient_rows(second_t, lambda i=index: logit_grad[:, 512 * i : 512 * i + 512], store)
    parts[2].start_pair()

    upper[...] = bf(dot_nt(logit_grad[...], readout_v[...]) * 0.5)
    back = dot_nt(upper[...], mixers_v[1])
    logits[:, 0:INNER] = back

    def coarse_rows(row):
        rows = pl.ds(row, STEP)
        back_rows = logits[rows, 0:INNER]
        for pair in range(2):
            wide2[1, pair, rows, :] = bf(back_rows * gelu_slope(inner2[pair, rows, :]))

    row_blocks(128, STEP, coarse_rows)
    edges = exchange_grads(wide2, send, after, before)
    parts[2].end_pair()
    parts[2].start_level(0)

    def store_coarse(y, x_hi, z, block):
        terms1[0, y, z, 2 * x_hi] = block

    gradient_rows(act2_t, lambda: flat(wide2[1]), store_coarse)
    finish_exchange(wide2, edges, seq, groups)
    mixed[0:2] = (
        dot_nt(flat(wide2[0]), kernels_v[1, 0])
        + dot_nt(flat(wide2[1]), kernels_v[1, 1])
        + dot_nt(flat(wide2[2]), kernels_v[1, 2])
    ).reshape(2, 128, CH)
    trunk_scale = math.sqrt(lax.axis_size("dp") * groups * 128) * 0.5

    def trunk_rows(row):
        rows = pl.ds(row, STEP)
        upper_rows = f32(upper[rows, :])
        for pair in range(2):
            grad = upper_rows + mixed[pair, rows, :] * gelu_slope(f32(first[pair, rows, :]))
            scaled = grad * trunk_scale
            for at in range(6):
                woven[at, pl.ds(2 * row + pair, STEP, stride=2), :] = scaled[:, 128 * at : 128 * at + 128]
            lower[pair, rows, :] = bf(grad * 0.5)

    row_blocks(128, STEP, trunk_rows)
    for at in range(6):
        trunk_out[:, 128 * at : 128 * at + 128] = woven[at]
    parts[2].relay_level(0)
    back = dot_nt(flat(lower[...]), mixers_v[0])
    mixed[0:2, :, 0:INNER] = back.reshape(2, 128, INNER)
    for pair in range(2):

        def fine_rows(row, pair=pair):
            rows = pl.ds(row, STEP)
            back_rows = mixed[pair, rows, 0:INNER]
            for side in range(2):
                wide1[1, 2 * pair + side, rows, :] = bf(back_rows * gelu_slope(inner1[2 * pair + side, rows, :]))

        row_blocks(128, STEP, fine_rows)

    edges = exchange_grads(wide1, send, after, before)
    parts[2].end_level(0)
    parts[2].start_level(1)

    def store_third(y, x_hi, z, block):
        terms0[1, 2 * x_hi + 1, y, z] = block

    def store_fifth(y, x_hi, z, block):
        terms1[1, y, z, 2 * x_hi] = block

    gradient_rows(act2_t, lambda: flat(wide2[0]), store_third)
    gradient_rows(act2_t, lambda: flat(wide2[2]), store_fifth)

    column = lax.broadcasted_iota(jnp.int32, (CH, INNER), 1)
    target_row = column + 12 * lax.shift_right_logical(column * 43691, 19)
    row_at = lax.broadcasted_iota(jnp.int32, (CH, INNER), 0)
    picks = jnp.where(row_at == target_row, 1.0, 0.0).astype(jnp.bfloat16)
    mixer_left[:, 0:512] = bf(dot_nt(picks, flat(gated1[...])))
    picks = jnp.where(row_at == target_row + 12, 1.0, 0.0).astype(jnp.bfloat16)
    mixer_left[:, 512:768] = bf(dot_nt(picks, flat(gated2[...])))
    for at in range(4):
        mixer_right[128 * at : 128 * at + 128] = lower[at // 2]
    for at in range(4, 6):
        mixer_right[128 * at : 128 * at + 128] = upper[...]
    for half in range(2):

        def store_mixer(y, x_hi, z, block, half=half):
            terms1[half, y, z, 2 * x_hi + 1] = block

        gradient_rows(mixer_left, lambda h=half: mixer_right[:, INNER * h : INNER * h + INNER], store_mixer)
    parts[1].start_pair()

    def fine_store(tap):
        def store(y, x_hi, z, block):
            terms0[tap % 2, 2 * x_hi + tap // 2, y, z] = block

        return store

    gradient_rows(act1_t, lambda: flat(wide1[1]), fine_store(1))
    finish_exchange(wide1, edges, seq, groups)
    parts[2].relay_level(1)
    gradient_rows(act1_t, lambda: flat(wide1[0]), fine_store(0))
    parts[1].end_pair()
    parts[1].start_level(0)
    gradient_rows(act1_t, lambda: flat(wide1[2]), fine_store(2))
    parts[0].start_pair()
    parts[2].end_level(1)
    parts[2].start_last()
    parts[1].relay_level(0)
    parts[0].end_pair()
    parts[0].start_level(0)
    readout_out[...] = parts[2].end_last()
    parts[1].end_level(0)
    parts[1].start_level(1)
    parts[0].relay_level(0)
    parts[1].relay_level(1)
    parts[0].end_level(0)
    parts[0].start_level(1)
    parts[1].end_level(1)
    parts[1].start_last()
    parts[0].relay_level(1)
    joined[dp, :, 384:768] = parts[1].end_last()
    parts[0].end_level(1)
    parts[0].start_last()
    joined[dp, :, 0:384] = parts[0].end_last()
    mine = joined.at[dp]
    last = [send(mine, mine, device) for device in group]
    for copy in last:
        copy.wait_recv()
    for index in range(4):

        @pl.when(dp == index)
        def _():
            low = 96 * index
            for tap in range(6):
                slot, start = (tap, low) if tap < 4 else (tap - 4, 384 + low)
                kernel_out[tap] = joined[slot, :, start : start + 96]
            slot, start = 2 + index // 2, 384 + 192 * (index % 2)
            mixer_out[0] = joined[slot, 0:12, start : start + 192]
            mixer_out[1] = joined[slot, 12:24, start : start + 192]

    send.finish()


N_REDUCE = 3 * (1 + 6 + 6 + 3) + 3 + 8


def blocks_and_gradients(landed, lane_position, length, targets, kernels, mixers, readout):
    vmem, anywhere = pl.BlockSpec(memory_space=pltpu.VMEM), pl.BlockSpec(memory_space=pl.ANY)
    bf16, single = jnp.bfloat16, jnp.float32
    return pl.pallas_call(
        blocks_kernel,
        out_shape=(
            jax.ShapeDtypeStruct((6, 24, 96), single),
            jax.ShapeDtypeStruct((2, 12, 192), single),
            jax.ShapeDtypeStruct((24, 512), single),
            jax.ShapeDtypeStruct((256, CH), single),
        ),
        in_specs=[vmem, vmem, pl.BlockSpec(memory_space=pltpu.SMEM)] + [anywhere] * 4,
        out_specs=[vmem] * 4,
        scratch_shapes=[
            pltpu.VMEM((2, 3, CH, INNER), bf16),
            pltpu.VMEM((2, INNER, CH), bf16),
            pltpu.VMEM((CH, 2048), bf16),
            pltpu.VMEM((128, 2048), jnp.int32),
            pltpu.SemaphoreType.DMA((5,)),
            pltpu.VMEM((4, 128, CH), bf16),
            pltpu.VMEM((4, 128, CH), bf16),
            pltpu.VMEM((4, 128, INNER), single),
            pltpu.VMEM((4, 128, INNER), bf16),
            pltpu.VMEM((4, 128, CH), single),
            pltpu.VMEM((2, 128, CH), bf16),
            pltpu.VMEM((2, 128, CH), bf16),
            pltpu.VMEM((2, 128, INNER), single),
            pltpu.VMEM((2, 128, INNER), bf16),
            pltpu.VMEM((128, CH), bf16),
            pltpu.VMEM((128, 2048), single),
            pltpu.VMEM((128, 2048), bf16),
            pltpu.VMEM((128, CH), bf16),
            pltpu.VMEM((6, 256, 128), single),
            pltpu.VMEM((3, 2, 128, INNER), bf16),
            pltpu.VMEM((3, 4, 128, INNER), bf16),
            pltpu.VMEM((2, 128, CH), bf16),
            pltpu.VMEM((CH, 512), bf16),
            pltpu.VMEM((CH, 256), bf16),
            pltpu.VMEM((CH, 128), bf16),
            pltpu.VMEM((CH, CH), bf16),
            pltpu.VMEM((CH, CH), bf16),
            pltpu.VMEM((2, 4, HALF, INNER), bf16),
            pltpu.VMEM((2, 4, HALF, INNER), bf16),
            pltpu.VMEM((2, 2, HALF, INNER), bf16),
            pltpu.VMEM((2, 2, HALF, INNER), bf16),
        ]
        + [pltpu.VMEM((2, 4, 4, 4, 24, width), bf16) for width in WIDTHS]
        + [s for width in WIDTHS for s in part_scratch(width)]
        + [
            pltpu.VMEM((4, 24, CH), single),
            pltpu.SemaphoreType.DMA((N_REDUCE,)),
            pltpu.SemaphoreType.DMA((N_REDUCE,)),
        ],
        compiler_params=pltpu.CompilerParams(
            collective_id=2, has_side_effects=True, vmem_limit_bytes=60 << 20
        ),
        name="blocks",
    )(landed, lane_position, length, targets, kernels, mixers, readout)


def shards(embeddings, layout, lengths, targets, projection, kernels, mixers, readout):
    row_count = embeddings.shape[2]
    block_rows = row_count // lax.axis_size("seq")
    column = lax.dynamic_index_in_dim(layout[0], lax.axis_index("seq"), axis=1, keepdims=False)
    lane_position = (
        column[:, None] * block_rows + jnp.arange(block_rows, dtype=jnp.int32)[None, :]
    ).reshape(1, row_count)
    landed = project_and_exchange(embeddings[0, 0], projection)
    kernel_total, mixer_total, readout_total, trunk_grad = blocks_and_gradients(
        landed, lane_position, lengths, targets[0], kernels, mixers, readout
    )
    return (kernel_total.reshape(2, 3, 24, 96), mixer_total, readout_total, trunk_grad[None])


def solution(mesh):
    placed = (
        P("dp", "seq", None, None),
        P("dp", None, None),
        P("dp"),
        P("dp", "seq", None),
        P("dp", None),
        P(),
        P(),
        P(),
    )
    return jax.shard_map(
        shards,
        mesh=mesh,
        in_specs=placed,
        out_specs=(
            P(None, None, "seq", "dp"),
            P(None, "seq", "dp"),
            P("seq", "dp"),
            P("dp", "seq", None),
        ),
        check_vma=False,
    )
```

```python
import math

import jax
import jax.numpy as jnp
from jax import lax
from jax.experimental import pallas as pl
from jax.experimental.pallas import tpu as pltpu
from jax.sharding import PartitionSpec as P

MESH = pl.DeviceIdType.MESH
CHUNK = 512
STAGES = ((0, 512, 96), (1280, 256, 64))
STAGE_ROWS = (1280, 768)
GROUPS = (
    (((0, 1, 2), 128), ((1, 2, 0), 128), ((2, 0, 1), 128)),
    (((0, 1, 2), 128), ((1, 2, 0), 128), ((2, 0, 1), 128)),
    (((1, 0, 2), 256), ((0, 1, 2), 256)),
)


def place():
    dp, seq = lax.axis_index("dp"), lax.axis_index("seq")
    core = lax.rem(dp, 2)
    x = lax.rem(lax.div(seq, 4), 2) * 2 + lax.div(dp, 2)
    return (x, lax.div(seq, 8), lax.rem(seq, 4)), core


def device_at(coords, core):
    x, y, z = coords
    return (lax.rem(x, 2) * 2 + core, y * 8 + lax.div(x, 2) * 4 + z)


def moved(coords, axis, step):
    out = list(coords)
    out[axis] = lax.rem(out[axis] + step, 4)
    return tuple(out)


class Sender:
    def __init__(self, send_sems, recv_sems):
        self.send_sems, self.recv_sems, self.copies = send_sems, recv_sems, []

    def __call__(self, src, dst, device):
        at = len(self.copies)
        copy = pltpu.make_async_remote_copy(
            src_ref=src,
            dst_ref=dst,
            send_sem=self.send_sems.at[at],
            recv_sem=self.recv_sems.at[at],
            device_id=device,
            device_id_type=MESH,
        )
        copy.start()
        self.copies.append(copy)
        return copy

    def finish(self):
        for copy in self.copies:
            copy.wait_send()


def greet(devices):
    barrier = pltpu.get_barrier_semaphore()
    for device in devices:
        pl.semaphore_signal(barrier, inc=1, device_id=device, device_id_type=MESH)
    pl.semaphore_wait(barrier, len(devices))


def f32(values):
    return values.astype(jnp.float32)


def project(emb, weights, emb_v, w_v, acc, rows_v, landed, coords, core, meet, pass_on, local_sems, send, a2a_send, a2a_recv):
    dp, seq = lax.axis_index("dp"), lax.axis_index("seq")
    groups = lax.axis_size("seq")
    depth = weights.shape[0]
    partner = device_at(coords, 1 - core)
    sides = (device_at(moved(coords, 0, 1), core), device_at(moved(coords, 0, 3), core))
    across = lax.rem(dp + 2, 4)
    order = (dp, dp + 1 - 2 * core, across, across + 1 - 2 * core)
    own_w = pltpu.make_async_copy(weights, w_v.at[dp], local_sems.at[4])
    own_w.start()

    def load(at):
        cols = pl.ds(pl.multiple_of(order[at] * depth, depth), depth)
        copy = pltpu.make_async_copy(emb.at[:, cols], emb_v.at[at % 2], local_sems.at[at])
        copy.start()
        return copy

    loads = [load(0), load(1)]
    meet()

    def piece(stage, axis, owner, side):
        base, direct, size = STAGES[stage]
        start = base + direct + 4 * size * (axis - 1)
        if side is None:
            return pl.ds(pl.multiple_of(start + size * owner, 32), size)
        return pl.ds(pl.multiple_of(start + size * owner + size // 2 * side, 16), size // 2)

    def straight(stage, side):
        base, direct, _ = STAGES[stage]
        return pl.ds(base + direct // 2 * side, direct // 2)

    crossing, direct = {}, {}
    for stage in range(2):
        for axis in (1, 2):
            for side in range(2):
                rows = piece(stage, axis, coords[axis], side)
                crossing[stage, axis, side] = send(weights.at[rows], w_v.at[dp, rows], sides[side])
    for stage in range(2):
        for side in range(2):
            rows = straight(stage, side)
            direct[stage, side] = send(weights.at[rows], w_v.at[dp, rows], sides[side])
    to_partner = send(weights, w_v.at[dp], partner)

    def accumulate(at, row, size):
        acc[...] += jnp.dot(
            emb_v[at % 2, :, pl.ds(pl.multiple_of(row, 128), size)],
            w_v[order[at], pl.ds(pl.multiple_of(row, 128), size), :],
            preferred_element_type=jnp.float32,
        )

    rings, relays = {}, {}

    def spread(stage):
        for axis in (1, 2):
            for side in range(2):
                crossing[stage, axis, side].wait_recv()
                block = w_v.at[across, piece(stage, axis, coords[axis], side)]
                for k in (2, 1, 3):
                    rings.setdefault((stage, axis, k), []).append(
                        send(block, block, device_at(moved(coords, axis, k), core))
                    )

    def relay(stage, axis, k):
        block = w_v.at[across, piece(stage, axis, lax.rem(coords[axis] + 4 - k, 4), None)]
        relays[stage, axis, k] = send(block, block, partner)

    def collect(stage):
        for axis in (1, 2):
            relay(stage, axis, 0)
        for side in range(2):
            direct[stage, side].wait_recv()
            block = w_v.at[across, straight(stage, side)]
            relays[stage, 0, side] = send(block, block, partner)
        for k in (1, 3, 2):
            for axis in (1, 2):
                for copy in rings[stage, axis, k]:
                    copy.wait_recv()
                relay(stage, axis, k)

    def take(stage):
        for key, copy in relays.items():
            if key[0] == stage:
                copy.wait_recv()

    acc[...] = jnp.zeros_like(acc)
    loads[0].wait()
    own_w.wait()

    @pl.loop(0, depth // CHUNK)
    def _(step):
        accumulate(0, step * CHUNK, CHUNK)

    loads.append(load(2))
    spread(0)
    pass_on()
    loads[1].wait()
    to_partner.wait_recv()
    accumulate(1, 0, 1024)
    spread(1)
    accumulate(1, 1024, 1024)
    loads.append(load(3))
    loads[2].wait()
    collect(0)
    accumulate(2, 0, STAGE_ROWS[0])
    loads[3].wait()
    take(0)
    accumulate(3, 0, STAGE_ROWS[0])
    collect(1)
    accumulate(2, STAGE_ROWS[0], STAGE_ROWS[1])
    take(1)

    def block_copy(off):
        there = lax.rem(seq + off, groups)
        return pltpu.make_async_remote_copy(
            src_ref=rows_v.at[there],
            dst_ref=landed.at[seq],
            send_sem=a2a_send.at[off],
            recv_sem=a2a_recv.at[off],
            device_id=(dp, there),
            device_id_type=MESH,
        )

    tail = pl.ds(STAGE_ROWS[0], STAGE_ROWS[1])
    total = acc[...] + jnp.dot(emb_v[1, :, tail], w_v[order[3], tail, :], preferred_element_type=jnp.float32)
    rows_v[...] = total.astype(jnp.bfloat16).reshape(rows_v.shape)
    return block_copy


class Part:
    def __init__(self, order, terms, scratch, send, coords, core):
        self.order, self.terms, self.send, self.coords, self.core = order, terms, send, coords, core
        self.pair, self.halves, self.acc2, self.next, self.acc3, self.last = scratch
        self.acc1 = self.pair

    def start_pair(self):
        self.pair_copy = self.send(
            self.terms.at[1 - self.core], self.pair, device_at(self.coords, 1 - self.core)
        )

    def start_first(self):
        self.pair_copy.wait_recv()

        @pl.loop(0, 4)
        def _(at):
            self.acc1[at] = (f32(self.terms[self.core, at]) + f32(self.pair[at])).astype(jnp.bfloat16)

        acc, halves = self.acc1, self.halves
        here = self.coords[self.order[0]]
        self.up, self.down = (device_at(moved(self.coords, self.order[0], k), self.core) for k in (1, 3))
        after, before, opposite = (lax.rem(here + k, 4) for k in (1, 3, 2))
        low, high = pl.ds(0, 2), pl.ds(2, 2)
        self.arrivals = [
            self.send(acc.at[opposite, low], halves.at[0], self.up),
            self.send(acc.at[opposite, high], halves.at[1], self.down),
            self.send(acc.at[before, low], halves.at[2], self.down),
            self.send(acc.at[after, high], halves.at[3], self.up),
        ]

    def relay_first(self):
        acc, halves, here = self.acc1, self.halves, self.coords[self.order[0]]
        after, before = (lax.rem(here + k, 4) for k in (1, 3))
        self.arrivals[0].wait_recv()
        acc[after, 0:2] = (f32(halves[0]) + f32(acc[after, 0:2])).astype(jnp.bfloat16)
        self.arrivals.append(self.send(acc.at[after, pl.ds(0, 2)], halves.at[4], self.up))
        self.arrivals[1].wait_recv()
        acc[before, 2:4] = (f32(halves[1]) + f32(acc[before, 2:4])).astype(jnp.bfloat16)
        self.arrivals.append(self.send(acc.at[before, pl.ds(2, 2)], halves.at[5], self.down))

    def end_first(self):
        acc, halves, here = self.acc1, self.halves, self.coords[self.order[0]]
        for copy in self.arrivals[2:]:
            copy.wait_recv()
        self.acc2[0:2] = (f32(acc[here, 0:2]) + f32(halves[2]) + f32(halves[4])).astype(jnp.bfloat16)
        self.acc2[2:4] = (f32(acc[here, 2:4]) + f32(halves[3]) + f32(halves[5])).astype(jnp.bfloat16)
        self.exchange(1, self.acc2, self.next)

    def exchange(self, number, acc, into):
        axis = self.order[number]
        here = self.coords[axis]
        self.arrivals = [
            self.send(
                acc.at[lax.rem(here + k, 4)],
                into.at[k - 1],
                device_at(moved(self.coords, axis, k), self.core),
            )
            for k in (2, 1, 3)
        ]

    def gathered(self, number, acc, into):
        for copy in self.arrivals:
            copy.wait_recv()
        here = self.coords[self.order[number]]
        return (f32(acc[here]) + f32(into[0])) + (f32(into[1]) + f32(into[2]))

    def end_second(self):
        self.acc3[...] = self.gathered(1, self.acc2, self.next).astype(jnp.bfloat16)
        self.exchange(2, self.acc3, self.last)

    def end_last(self):
        return self.gathered(2, self.acc3, self.last)


def part_scratch(width):
    unit = (24, width)
    return [
        pltpu.VMEM(shape + unit, jnp.bfloat16)
        for shape in ((4, 4, 4), (6, 2, 4), (4, 4), (3, 4), (4,), (3,))
    ]


def gelu(values):
    return 0.5 * values * (1.0 + lax.erf(values * (1.0 / math.sqrt(2.0))))


def gelu_slope(values):
    cumulative = 0.5 * (1.0 + lax.erf(values * (1.0 / math.sqrt(2.0))))
    density = jnp.exp(-0.5 * values * values) * (1.0 / math.sqrt(2.0 * math.pi))
    return cumulative + values * density


def bf(values):
    return values.astype(jnp.bfloat16)


def dot(left, right):
    return jnp.dot(left, right, preferred_element_type=jnp.float32)


def dot_nt(left, right):
    return lax.dot_general(
        left, right, (((1,), (1,)), ((), ())), preferred_element_type=jnp.float32
    )


def flat(values):
    return values.reshape(-1, values.shape[-1])


def row_blocks(count, step, body):
    @pl.loop(0, count // step)
    def _(at):
        body(pl.multiple_of(at * step, step))


STEP = 16
HALF = 64
INNER = 384
CH = 768


def conv_forward(act, kernel, inner, edge_out, edge_in, send, after, before, seq, groups):
    low, high = flat(act[:, 0:HALF, :]), flat(act[:, HALF:128, :])
    shape = (act.shape[0], HALF, INNER)
    edge_out[0] = bf(dot(high, kernel[0])).reshape(shape)
    from_before = send(edge_out.at[0], edge_in.at[0], after)
    edge_out[1] = bf(dot(low, kernel[2])).reshape(shape)
    from_after = send(edge_out.at[1], edge_in.at[1], before)
    inner[:, 0:HALF, :] = (dot(low, kernel[1]) + dot(high, kernel[2])).reshape(shape)
    inner[:, HALF:128, :] = (dot(high, kernel[1]) + dot(low, kernel[0])).reshape(shape)
    return from_before, from_after


def finish_inner(inner, gated, edge_in, copies, seq, groups):
    copies[0].wait_recv()
    copies[1].wait_recv()
    keeps = (jnp.where(seq == 0, 0.0, 1.0), jnp.where(seq == groups - 1, 0.0, 1.0))
    for side in range(2):

        @pl.loop(0, inner.shape[0])
        def _(group):
            for row in range(0, HALF, STEP):
                rows = slice(side * HALF + row, side * HALF + row + STEP)
                total = inner[group, rows, :] + f32(edge_in[side, group, row : row + STEP, :]) * keeps[side]
                inner[group, rows, :] = total
                gated[group, rows, :] = bf(gelu(total))


def exchange_grads(wide, send, after, before):
    from_after = send(wide.at[1, :, pl.ds(0, HALF)], wide.at[0, :, pl.ds(HALF, HALF)], before)
    from_before = send(wide.at[1, :, pl.ds(HALF, HALF)], wide.at[2, :, pl.ds(0, HALF)], after)
    wide[0, :, 0:HALF, :] = wide[1, :, HALF:128, :]
    wide[2, :, HALF:128, :] = wide[1, :, 0:HALF, :]
    return from_after, from_before


def finish_exchange(wide, copies, seq, groups):
    copies[0].wait_recv()
    copies[1].wait_recv()
    zeros = jnp.zeros((wide.shape[1], HALF, INNER), jnp.bfloat16)

    @pl.when(seq == groups - 1)
    def _():
        wide[0, :, HALF:128, :] = zeros

    @pl.when(seq == 0)
    def _():
        wide[2, :, 0:HALF, :] = zeros


def gradient_rows(transposed, right, store):
    @pl.loop(0, 4)
    def _(y):
        result = dot(transposed[pl.ds(pl.multiple_of(y * 192, 64), 192), :], right())
        for x_hi in range(2):
            for z in range(4):
                row = 24 * (4 * x_hi + z)
                store(y, x_hi, z, bf(result[row : row + 24]))


def step_kernel(
    emb, weights, lane_position, length_ref, targets, kernels, mixers, readout,
    joined_out, readout_out, woven,
    emb_v, w_v, total, rows_v, landed, load_sems, a2a_send, a2a_recv, ready,
    kernels_v, mixers_v, readout_v, targets_v, local_sems,
    hid, act1, inner1, gated1, mixed, first, act2, inner2, gated2, second, logits, logit_grad,
    upper, wide2, wide1, lower, act1_t, act2_t, second_t, mixer_left, mixer_right,
    edge1_out, edge1_in, edge2_out, edge2_in, *rest
):
    terms, parts_scratch, (joined, send_sems, recv_sems) = rest[:N_PARTS], rest[N_PARTS:-3], rest[-3:]
    coords, core = place()
    dp, seq = lax.axis_index("dp"), lax.axis_index("seq")
    groups = lax.axis_size("seq")
    loads = []
    for at, (src, dst) in enumerate(
        (
            (kernels.at[0], kernels_v.at[0]),
            (mixers, mixers_v),
            (kernels.at[1], kernels_v.at[1]),
            (readout, readout_v),
            (targets, targets_v),
        )
    ):
        loads.append(pltpu.make_async_copy(src, dst, local_sems.at[at]))
    after, before = (dp, lax.rem(seq + 1, groups)), (dp, lax.rem(seq + groups - 1, groups))
    send = Sender(send_sems, recv_sems)
    parts = []
    for members in GROUPS:
        parts.append([])
        for order, _ in members:
            at = sum(len(group) for group in parts)
            parts[-1].append(Part(order, terms[at], parts_scratch[6 * at : 6 * at + 6], send, coords, core))

    def put(number, unit):
        def store(y, x_hi, z, block):
            spot = (2 * x_hi + unit // 2, y, z)
            start = 0
            for part, (order, width) in zip(parts[number], GROUPS[number]):
                part.terms[unit % 2, spot[order[0]], spot[order[1]], spot[order[2]]] = block[:, start : start + width]
                start += width

        return store

    def each(number, step):
        return [getattr(part, step)() for part in parts[number]]

    def gather_last(number):
        return jnp.concatenate(each(number, "end_last"), axis=1)

    pair_x = (coords[0] + 1 - 2 * lax.rem(coords[0], 2),) + coords[1:]
    partner = device_at(coords, 1 - core)
    group = [partner, device_at(pair_x, core), device_at(pair_x, 1 - core)]

    def meet():
        greet(
            [device_at(moved(coords, axis, k), core) for axis in range(3) for k in (1, 2, 3)]
            + [partner, device_at(pair_x, 1 - core), after, before]
        )
        for k in (1, 2, 3):
            pl.semaphore_signal(
                ready.at[0], inc=1, device_id=device_at(moved(coords, 1, k), core), device_id_type=MESH
            )

    def pass_on():
        for copy in loads:
            copy.start()
        pl.semaphore_wait(ready.at[0], 3)
        pl.semaphore_signal(
            ready.at[1], inc=1, device_id=device_at(moved(coords, 0, 2), core), device_id_type=MESH
        )

    block_copy = project(
        emb, weights, emb_v, w_v, total, rows_v, landed, coords, core, meet, pass_on, load_sems, send, a2a_send, a2a_recv
    )
    length = length_ref[0]

    pl.semaphore_wait(ready.at[1], 1)

    @pl.loop(1, groups)
    def _(off):
        block_copy(off).start()

    landed[seq] = rows_v[seq]

    @pl.loop(1, groups)
    def _(off):
        block_copy(off).wait()

    blocks = flat(landed[...])
    for group_at in range(4):
        spot = 4 * lax.broadcasted_iota(jnp.int32, (128, 512), 0) + group_at
        chosen = (lane_position[...] == spot) & (spot + seq * 512 < length)
        hid[group_at] = bf(dot(jnp.where(chosen, 1.0, 0.0).astype(jnp.bfloat16), blocks))

    for group_at in range(4):

        def gelu_rows(row, group_at=group_at):
            act1[group_at, pl.ds(row, STEP), :] = bf(gelu(f32(hid[group_at, pl.ds(row, STEP), :])))

        row_blocks(128, STEP, gelu_rows)

    loads[0].wait()
    edges = conv_forward(act1, kernels_v.at[0], inner1, edge1_out, edge1_in, send, after, before, seq, groups)
    act1_t[...] = flat(act1[...]).T
    finish_inner(inner1, gated1, edge1_in, edges, seq, groups)
    loads[1].wait()
    mixed[...] = dot(flat(gated1[...]), mixers_v[0]).reshape(mixed.shape)
    for pair in range(2):

        def pool_rows(row, pair=pair):
            rows = pl.ds(row, STEP)
            total = (f32(hid[2 * pair, rows, :]) + mixed[2 * pair, rows, :]) + (
                f32(hid[2 * pair + 1, rows, :]) + mixed[2 * pair + 1, rows, :]
            )
            pooled = bf(total * 0.5)
            first[pair, rows, :] = pooled
            act2[pair, rows, :] = bf(gelu(f32(pooled)))

        row_blocks(128, STEP, pool_rows)

    loads[2].wait()
    edges = conv_forward(act2, kernels_v.at[1], inner2, edge2_out, edge2_in, send, after, before, seq, groups)
    act2_t[...] = flat(act2[...]).T
    finish_inner(inner2, gated2, edge2_in, edges, seq, groups)
    mixed[0:2] = dot(flat(gated2[...]), mixers_v[1]).reshape(2, 128, CH)

    def pool_again(row):
        rows = pl.ds(row, STEP)
        total = (f32(first[0, rows, :]) + mixed[0, rows, :]) + (f32(first[1, rows, :]) + mixed[1, rows, :])
        second[rows, :] = bf(total * 0.5)

    row_blocks(128, STEP, pool_again)
    loads[3].wait()
    loads[4].wait()
    logits[...] = dot(second[...], readout_v[...])
    loss_scale = 2.0 / math.sqrt(lax.axis_size("dp") * groups * 128)

    def loss_rows(row):
        rows = pl.ds(row, 8)
        values = logits[rows, :]
        small = jnp.exp(-jnp.abs(values))
        softplus = jnp.maximum(values, 0.0) + jnp.log1p(small)
        sigmoid = jnp.where(values >= 0.0, 1.0, small) / (1.0 + small)
        bins = seq * 128 + row + lax.broadcasted_iota(jnp.int32, (8, 1), 0)
        valid = jnp.where(bins * 4 < length, loss_scale, 0.0)
        mixed_rows = valid * (softplus - targets_v[rows, :].astype(jnp.float32)) * sigmoid
        logits[rows, :] = mixed_rows

    row_blocks(128, 8, loss_rows)
    logit_grad[...] = bf(logits[...])
    second_t[...] = second[...].T
    for index in range(4):
        gradient_rows(second_t, lambda i=index: logit_grad[:, 512 * i : 512 * i + 512], put(2, index))
    each(2, "start_pair")

    upper[...] = bf(dot_nt(logit_grad[...], readout_v[...]) * 0.5)
    back = dot_nt(upper[...], mixers_v[1])
    logits[:, 0:INNER] = back

    def coarse_rows(row):
        rows = pl.ds(row, STEP)
        back_rows = logits[rows, 0:INNER]
        for pair in range(2):
            wide2[1, pair, rows, :] = bf(back_rows * gelu_slope(inner2[pair, rows, :]))

    row_blocks(128, STEP, coarse_rows)
    edges = exchange_grads(wide2, send, after, before)
    each(2, "start_first")
    gradient_rows(act2_t, lambda: flat(wide2[1]), put(1, 1))
    row_at = lax.broadcasted_iota(jnp.int32, (CH, INNER), 0)
    column = lax.broadcasted_iota(jnp.int32, (CH, INNER), 1)
    target_row = column + 12 * lax.shift_right_logical(column * 43691, 19)
    for half in range(2):
        picks = jnp.where(row_at == target_row + 12 * half, 1.0, 0.0).astype(jnp.bfloat16)
        mixer_left[:, 256 * half : 256 * half + 256] = bf(dot_nt(picks, flat(gated2[...])))
        for pair in range(2):
            row = 256 * half + 128 * pair
            mixer_right[row : row + 128] = upper[:, INNER * half : INNER * half + INNER]
    gradient_rows(mixer_left.at[:, pl.ds(0, 512)], lambda: mixer_right[0:512], put(1, 3))
    finish_exchange(wide2, edges, seq, groups)
    gradient_rows(act2_t, lambda: flat(wide2[0]), put(1, 0))
    gradient_rows(act2_t, lambda: flat(wide2[2]), put(1, 2))
    each(1, "start_pair")
    mixed[0:2] = (
        dot_nt(flat(wide2[0]), kernels_v[1, 0])
        + dot_nt(flat(wide2[1]), kernels_v[1, 1])
        + dot_nt(flat(wide2[2]), kernels_v[1, 2])
    ).reshape(2, 128, CH)
    trunk_scale = math.sqrt(lax.axis_size("dp") * groups * 128) * 0.5

    def trunk_rows(row):
        rows = pl.ds(row, STEP)
        upper_rows = f32(upper[rows, :])
        for pair in range(2):
            grad = upper_rows + mixed[pair, rows, :] * gelu_slope(f32(first[pair, rows, :]))
            scaled = grad * trunk_scale
            for at in range(6):
                woven[at, pl.ds(2 * row + pair, STEP, stride=2), :] = scaled[:, 128 * at : 128 * at + 128]
            lower[pair, rows, :] = bf(grad * 0.5)

    row_blocks(128, STEP, trunk_rows)
    each(2, "relay_first")
    each(1, "start_first")
    back = dot_nt(flat(lower[...]), mixers_v[0])
    mixed[0:2, :, 0:INNER] = back.reshape(2, 128, INNER)
    for pair in range(2):

        def fine_rows(row, pair=pair):
            rows = pl.ds(row, STEP)
            back_rows = mixed[pair, rows, 0:INNER]
            for side in range(2):
                wide1[1, 2 * pair + side, rows, :] = bf(back_rows * gelu_slope(inner1[2 * pair + side, rows, :]))

        row_blocks(128, STEP, fine_rows)

    edges = exchange_grads(wide1, send, after, before)
    each(2, "end_first")
    each(1, "relay_first")
    gradient_rows(act1_t, lambda: flat(wide1[1]), put(0, 1))
    for half in range(2):
        picks = jnp.where(row_at == target_row + 12 * half, 1.0, 0.0).astype(jnp.bfloat16)
        mixer_left[:, 512 * half : 512 * half + 512] = bf(dot_nt(picks, flat(gated1[...])))
        for group_at in range(4):
            row = 512 * half + 128 * group_at
            mixer_right[row : row + 128] = lower[group_at // 2, :, INNER * half : INNER * half + INNER]
    gradient_rows(mixer_left, lambda: mixer_right[...], put(0, 3))
    each(1, "end_first")
    finish_exchange(wide1, edges, seq, groups)
    gradient_rows(act1_t, lambda: flat(wide1[0]), put(0, 0))
    gradient_rows(act1_t, lambda: flat(wide1[2]), put(0, 2))
    each(0, "start_pair")
    each(2, "end_second")
    each(1, "end_second")
    each(0, "start_first")
    readout_out[...] = gather_last(2)
    each(0, "relay_first")
    joined[dp, :, 384:768] = gather_last(1)
    each(0, "end_first")
    each(0, "end_second")
    joined[dp, :, 0:384] = gather_last(0)
    mine = joined.at[dp]
    last = [send(mine, mine, device) for device in group]
    for copy in last:
        copy.wait_recv()
    joined_out[...] = joined[...]
    send.finish()


N_PARTS = sum(len(group) for group in GROUPS)
N_GATHER = 8 + 4 + 1 + 24 + 16 + 4
N_COPIES = N_GATHER + N_PARTS * (1 + 6 + 3 + 3) + 3 + 8


def finish_kernel(joined, readout_part, woven, kernel_out, mixer_out, readout_out, trunk_out):
    dp = lax.axis_index("dp")
    for index in range(4):

        @pl.when(dp == index)
        def _():
            low = 96 * index
            for tap in range(6):
                start = 384 * (tap // 3) + low
                kernel_out[tap // 3, tap % 3] = joined[tap % 3, :, start : start + 96]
            row, low = 12 * (index // 2), 192 * (index % 2)
            for block in range(2):
                start = 384 * block + low
                mixer_out[block] = joined[3, row : row + 12, start : start + 192]

    readout_out[...] = readout_part[...]
    for at in range(6):
        trunk_out[:, 128 * at : 128 * at + 128] = woven[at]


def write_outputs(joined, readout_part, woven):
    vmem, single = pl.BlockSpec(memory_space=pltpu.VMEM), jnp.float32
    return pl.pallas_call(
        finish_kernel,
        out_shape=(
            jax.ShapeDtypeStruct((2, 3, 24, 96), single),
            jax.ShapeDtypeStruct((2, 12, 192), single),
            jax.ShapeDtypeStruct((24, 512), single),
            jax.ShapeDtypeStruct((256, CH), single),
        ),
        in_specs=[vmem] * 3,
        out_specs=[vmem] * 4,
        name="outputs",
    )(joined, readout_part, woven)


def step(emb, weights, lane_position, length, targets, kernels, mixers, readout):
    vmem, anywhere = pl.BlockSpec(memory_space=pltpu.VMEM), pl.BlockSpec(memory_space=pl.ANY)
    bf16, single = jnp.bfloat16, jnp.float32
    rows, depth, groups = emb.shape[0], weights.shape[0], lax.axis_size("seq")
    blocks = (groups, rows // groups, CH)
    return pl.pallas_call(
        step_kernel,
        out_shape=(
            jax.ShapeDtypeStruct((4, 24, CH), single),
            jax.ShapeDtypeStruct((24, 512), single),
            jax.ShapeDtypeStruct((6, 256, 128), single),
        ),
        in_specs=[anywhere, anywhere, vmem, pl.BlockSpec(memory_space=pltpu.SMEM)] + [anywhere] * 4,
        out_specs=[vmem] * 3,
        scratch_shapes=[
            pltpu.VMEM((2, rows, depth), bf16),
            pltpu.VMEM((4, depth, CH), bf16),
            pltpu.VMEM((rows, CH), single),
            pltpu.VMEM(blocks, bf16),
            pltpu.VMEM(blocks, bf16),
            pltpu.SemaphoreType.DMA((5,)),
            pltpu.SemaphoreType.DMA((groups,)),
            pltpu.SemaphoreType.DMA((groups,)),
            pltpu.SemaphoreType.REGULAR((2,)),
            pltpu.VMEM((2, 3, CH, INNER), bf16),
            pltpu.VMEM((2, INNER, CH), bf16),
            pltpu.VMEM((CH, 2048), bf16),
            pltpu.VMEM((128, 2048), jnp.int32),
            pltpu.SemaphoreType.DMA((5,)),
            pltpu.VMEM((4, 128, CH), bf16),
            pltpu.VMEM((4, 128, CH), bf16),
            pltpu.VMEM((4, 128, INNER), single),
            pltpu.VMEM((4, 128, INNER), bf16),
            pltpu.VMEM((4, 128, CH), single),
            pltpu.VMEM((2, 128, CH), bf16),
            pltpu.VMEM((2, 128, CH), bf16),
            pltpu.VMEM((2, 128, INNER), single),
            pltpu.VMEM((2, 128, INNER), bf16),
            pltpu.VMEM((128, CH), bf16),
            pltpu.VMEM((128, 2048), single),
            pltpu.VMEM((128, 2048), bf16),
            pltpu.VMEM((128, CH), bf16),
            pltpu.VMEM((3, 2, 128, INNER), bf16),
            pltpu.VMEM((3, 4, 128, INNER), bf16),
            pltpu.VMEM((2, 128, CH), bf16),
            pltpu.VMEM((CH, 512), bf16),
            pltpu.VMEM((CH, 256), bf16),
            pltpu.VMEM((CH, 128), bf16),
            pltpu.VMEM((CH, 1024), bf16),
            pltpu.VMEM((1024, INNER), bf16),
            pltpu.VMEM((2, 4, HALF, INNER), bf16),
            pltpu.VMEM((2, 4, HALF, INNER), bf16),
            pltpu.VMEM((2, 2, HALF, INNER), bf16),
            pltpu.VMEM((2, 2, HALF, INNER), bf16),
        ]
        + [pltpu.VMEM((2, 4, 4, 4, 24, width), bf16) for group in GROUPS for _, width in group]
        + [s for group in GROUPS for _, width in group for s in part_scratch(width)]
        + [
            pltpu.VMEM((4, 24, CH), single),
            pltpu.SemaphoreType.DMA((N_COPIES,)),
            pltpu.SemaphoreType.DMA((N_COPIES,)),
        ],
        compiler_params=pltpu.CompilerParams(
            collective_id=0, has_side_effects=True, vmem_limit_bytes=66 * 10**6
        ),
        name="step",
    )(emb, weights, lane_position, length, targets, kernels, mixers, readout)


def shards(embeddings, layout, lengths, targets, projection, kernels, mixers, readout):
    row_count = embeddings.shape[2]
    block_rows = row_count // lax.axis_size("seq")
    column = lax.dynamic_index_in_dim(layout[0], lax.axis_index("seq"), axis=1, keepdims=False)
    lane_position = (
        column[:, None] * block_rows + jnp.arange(block_rows, dtype=jnp.int32)[None, :]
    ).reshape(1, row_count)
    kernel_total, mixer_total, readout_total, trunk_grad = write_outputs(
        *step(embeddings[0, 0], projection, lane_position, lengths, targets[0], kernels, mixers, readout)
    )
    return (kernel_total, mixer_total, readout_total, trunk_grad[None])


def solution(mesh):
    placed = (
        P("dp", "seq", None, None),
        P("dp", None, None),
        P("dp"),
        P("dp", "seq", None),
        P("dp", None),
        P(),
        P(),
        P(),
    )
    return jax.shard_map(
        shards,
        mesh=mesh,
        in_specs=placed,
        out_specs=(
            P(None, None, "seq", "dp"),
            P(None, "seq", "dp"),
            P("seq", "dp"),
            P("dp", "seq", None),
        ),
        check_vma=False,
    )
```

```python
import math

import jax
import jax.numpy as jnp
from jax import lax
from jax.experimental import pallas as pl
from jax.experimental.pallas import tpu as pltpu
from jax.sharding import PartitionSpec as P

MESH = pl.DeviceIdType.MESH
CHUNK = 512
STAGES = ((0, 512, 96), (1280, 256, 64))
STAGE_ROWS = (1280, 768)
GROUPS = (
    (((0, 1, 2), 128), ((1, 2, 0), 128), ((2, 0, 1), 128)),
    (((0, 1, 2), 128), ((1, 0, 2), 256)),
    (((1, 0, 2), 256), ((0, 1, 2), 256)),
)


def place():
    dp, seq = lax.axis_index("dp"), lax.axis_index("seq")
    core = lax.rem(dp, 2)
    x = lax.rem(lax.div(seq, 4), 2) * 2 + lax.div(dp, 2)
    return (x, lax.div(seq, 8), lax.rem(seq, 4)), core


def device_at(coords, core):
    x, y, z = coords
    return (lax.rem(x, 2) * 2 + core, y * 8 + lax.div(x, 2) * 4 + z)


def moved(coords, axis, step):
    out = list(coords)
    out[axis] = lax.rem(out[axis] + step, 4)
    return tuple(out)


class Sender:
    def __init__(self, send_sems, recv_sems):
        self.send_sems, self.recv_sems, self.copies = send_sems, recv_sems, []

    def __call__(self, src, dst, device):
        at = len(self.copies)
        copy = pltpu.make_async_remote_copy(
            src_ref=src,
            dst_ref=dst,
            send_sem=self.send_sems.at[at],
            recv_sem=self.recv_sems.at[at],
            device_id=device,
            device_id_type=MESH,
        )
        copy.start()
        self.copies.append(copy)
        return copy

    def finish(self):
        for copy in self.copies:
            copy.wait_send()


def greet(devices):
    barrier = pltpu.get_barrier_semaphore()
    for device in devices:
        pl.semaphore_signal(barrier, inc=1, device_id=device, device_id_type=MESH)
    pl.semaphore_wait(barrier, len(devices))


def f32(values):
    return values.astype(jnp.float32)


def project(emb, weights, emb_v, w_v, acc, rows_v, landed, coords, core, meet, pass_on, local_sems, send, a2a_send, a2a_recv):
    dp, seq = lax.axis_index("dp"), lax.axis_index("seq")
    groups = lax.axis_size("seq")
    depth = weights.shape[0]
    partner = device_at(coords, 1 - core)
    sides = (device_at(moved(coords, 0, 1), core), device_at(moved(coords, 0, 3), core))
    across = lax.rem(dp + 2, 4)
    order = (dp, dp + 1 - 2 * core, across, across + 1 - 2 * core)
    own_w = pltpu.make_async_copy(weights, w_v.at[dp], local_sems.at[4])
    own_w.start()

    def load(at):
        cols = pl.ds(pl.multiple_of(order[at] * depth, depth), depth)
        copy = pltpu.make_async_copy(emb.at[:, cols], emb_v.at[at % 2], local_sems.at[at])
        copy.start()
        return copy

    loads = [load(0), load(1)]
    meet()

    def piece(stage, axis, owner, side):
        base, direct, size = STAGES[stage]
        start = base + direct + 4 * size * (axis - 1)
        if side is None:
            return pl.ds(pl.multiple_of(start + size * owner, 32), size)
        return pl.ds(pl.multiple_of(start + size * owner + size // 2 * side, 16), size // 2)

    def straight(stage, side):
        base, direct, _ = STAGES[stage]
        return pl.ds(base + direct // 2 * side, direct // 2)

    crossing, direct = {}, {}
    for stage in range(2):
        for axis in (1, 2):
            for side in range(2):
                rows = piece(stage, axis, coords[axis], side)
                crossing[stage, axis, side] = send(weights.at[rows], w_v.at[dp, rows], sides[side])
    for stage in range(2):
        for side in range(2):
            rows = straight(stage, side)
            direct[stage, side] = send(weights.at[rows], w_v.at[dp, rows], sides[side])
    to_partner = send(weights, w_v.at[dp], partner)

    def accumulate(at, row, size):
        acc[...] += jnp.dot(
            emb_v[at % 2, :, pl.ds(pl.multiple_of(row, 128), size)],
            w_v[order[at], pl.ds(pl.multiple_of(row, 128), size), :],
            preferred_element_type=jnp.float32,
        )

    rings, relays = {}, {}

    def spread(stage):
        for axis in (1, 2):
            for side in range(2):
                crossing[stage, axis, side].wait_recv()
                block = w_v.at[across, piece(stage, axis, coords[axis], side)]
                for k in (2, 1, 3):
                    rings.setdefault((stage, axis, k), []).append(
                        send(block, block, device_at(moved(coords, axis, k), core))
                    )

    def relay(stage, axis, k):
        block = w_v.at[across, piece(stage, axis, lax.rem(coords[axis] + 4 - k, 4), None)]
        relays[stage, axis, k] = send(block, block, partner)

    def collect(stage):
        for axis in (1, 2):
            relay(stage, axis, 0)
        for side in range(2):
            direct[stage, side].wait_recv()
            block = w_v.at[across, straight(stage, side)]
            relays[stage, 0, side] = send(block, block, partner)
        for k in (1, 3, 2):
            for axis in (1, 2):
                for copy in rings[stage, axis, k]:
                    copy.wait_recv()
                relay(stage, axis, k)

    def take(stage):
        for key, copy in relays.items():
            if key[0] == stage:
                copy.wait_recv()

    acc[...] = jnp.zeros_like(acc)
    loads[0].wait()
    own_w.wait()

    @pl.loop(0, depth // CHUNK)
    def _(step):
        accumulate(0, step * CHUNK, CHUNK)

    loads.append(load(2))
    spread(0)
    pass_on()
    loads[1].wait()
    to_partner.wait_recv()
    accumulate(1, 0, 1024)
    spread(1)
    accumulate(1, 1024, 1024)
    loads.append(load(3))
    loads[2].wait()
    collect(0)
    accumulate(2, 0, STAGE_ROWS[0])
    loads[3].wait()
    take(0)
    accumulate(3, 0, STAGE_ROWS[0])
    collect(1)
    accumulate(2, STAGE_ROWS[0], STAGE_ROWS[1])
    take(1)

    def block_copy(off):
        there = lax.rem(seq + off, groups)
        return pltpu.make_async_remote_copy(
            src_ref=rows_v.at[there],
            dst_ref=landed.at[seq],
            send_sem=a2a_send.at[off],
            recv_sem=a2a_recv.at[off],
            device_id=(dp, there),
            device_id_type=MESH,
        )

    tail = pl.ds(STAGE_ROWS[0], STAGE_ROWS[1])
    total = acc[...] + jnp.dot(emb_v[1, :, tail], w_v[order[3], tail, :], preferred_element_type=jnp.float32)
    rows_v[...] = total.astype(jnp.bfloat16).reshape(rows_v.shape)
    return block_copy


class Part:
    def __init__(self, order, terms, scratch, send, coords, core):
        self.order, self.terms, self.send, self.coords, self.core = order, terms, send, coords, core
        self.pair, self.halves, self.acc2, self.next, self.acc3, self.last = scratch
        self.acc1 = self.pair

    def start_pair(self):
        self.pair_copy = self.send(
            self.terms.at[1 - self.core], self.pair, device_at(self.coords, 1 - self.core)
        )

    def start_first(self):
        self.pair_copy.wait_recv()

        @pl.loop(0, 4)
        def _(at):
            self.acc1[at] = self.terms[self.core, at] + self.pair[at]

        acc, halves = self.acc1, self.halves
        here = self.coords[self.order[0]]
        self.up, self.down = (device_at(moved(self.coords, self.order[0], k), self.core) for k in (1, 3))
        after, before, opposite = (lax.rem(here + k, 4) for k in (1, 3, 2))
        low, high = pl.ds(0, 2), pl.ds(2, 2)
        self.arrivals = [
            self.send(acc.at[opposite, low], halves.at[0], self.up),
            self.send(acc.at[opposite, high], halves.at[1], self.down),
            self.send(acc.at[before, low], halves.at[2], self.down),
            self.send(acc.at[after, high], halves.at[3], self.up),
        ]

    def relay_first(self):
        acc, halves, here = self.acc1, self.halves, self.coords[self.order[0]]
        after, before = (lax.rem(here + k, 4) for k in (1, 3))
        self.arrivals[0].wait_recv()
        acc[after, 0:2] = halves[0] + acc[after, 0:2]
        self.arrivals.append(self.send(acc.at[after, pl.ds(0, 2)], halves.at[4], self.up))
        self.arrivals[1].wait_recv()
        acc[before, 2:4] = halves[1] + acc[before, 2:4]
        self.arrivals.append(self.send(acc.at[before, pl.ds(2, 2)], halves.at[5], self.down))

    def end_first(self):
        acc, halves, here = self.acc1, self.halves, self.coords[self.order[0]]
        for copy in self.arrivals[2:]:
            copy.wait_recv()
        self.acc2[0:2] = (f32(acc[here, 0:2]) + f32(halves[2]) + f32(halves[4])).astype(jnp.bfloat16)
        self.acc2[2:4] = (f32(acc[here, 2:4]) + f32(halves[3]) + f32(halves[5])).astype(jnp.bfloat16)
        self.exchange(1, self.acc2, self.next)

    def exchange(self, number, acc, into):
        axis = self.order[number]
        here = self.coords[axis]
        self.arrivals = [
            self.send(
                acc.at[lax.rem(here + k, 4)],
                into.at[k - 1],
                device_at(moved(self.coords, axis, k), self.core),
            )
            for k in (2, 1, 3)
        ]

    def gathered(self, number, acc, into):
        for copy in self.arrivals:
            copy.wait_recv()
        here = self.coords[self.order[number]]
        return (f32(acc[here]) + f32(into[0])) + (f32(into[1]) + f32(into[2]))

    def end_second(self):
        self.acc3[...] = self.gathered(1, self.acc2, self.next).astype(jnp.bfloat16)
        self.exchange(2, self.acc3, self.last)

    def end_last(self):
        return self.gathered(2, self.acc3, self.last)


def part_scratch(width):
    unit = (24, width)
    return [
        pltpu.VMEM(shape + unit, jnp.bfloat16)
        for shape in ((4, 4, 4), (6, 2, 4), (4, 4), (3, 4), (4,), (3,))
    ]


def gelu(values):
    return 0.5 * values * (1.0 + lax.erf(values * (1.0 / math.sqrt(2.0))))


def gelu_slope(values):
    cumulative = 0.5 * (1.0 + lax.erf(values * (1.0 / math.sqrt(2.0))))
    density = jnp.exp(-0.5 * values * values) * (1.0 / math.sqrt(2.0 * math.pi))
    return cumulative + values * density


def bf(values):
    return values.astype(jnp.bfloat16)


def dot(left, right):
    return jnp.dot(left, right, preferred_element_type=jnp.float32)


def dot_nt(left, right):
    return lax.dot_general(
        left, right, (((1,), (1,)), ((), ())), preferred_element_type=jnp.float32
    )


def flat(values):
    return values.reshape(-1, values.shape[-1])


def row_blocks(count, step, body):
    @pl.loop(0, count // step)
    def _(at):
        body(pl.multiple_of(at * step, step))


STEP = 16
HALF = 64
INNER = 384
CH = 768


def conv_forward(act, kernel, inner, edge_out, edge_in, send, after, before, seq, groups):
    low, high = flat(act[:, 0:HALF, :]), flat(act[:, HALF:128, :])
    shape = (act.shape[0], HALF, INNER)
    edge_out[0] = bf(dot(high, kernel[0])).reshape(shape)
    from_before = send(edge_out.at[0], edge_in.at[0], after)
    edge_out[1] = bf(dot(low, kernel[2])).reshape(shape)
    from_after = send(edge_out.at[1], edge_in.at[1], before)
    inner[:, 0:HALF, :] = (dot(low, kernel[1]) + dot(high, kernel[2])).reshape(shape)
    inner[:, HALF:128, :] = (dot(high, kernel[1]) + dot(low, kernel[0])).reshape(shape)
    return from_before, from_after


def finish_inner(inner, gated, edge_in, copies, seq, groups):
    copies[0].wait_recv()
    copies[1].wait_recv()
    keeps = (jnp.where(seq == 0, 0.0, 1.0), jnp.where(seq == groups - 1, 0.0, 1.0))
    for side in range(2):

        @pl.loop(0, inner.shape[0])
        def _(group):
            for row in range(0, HALF, STEP):
                rows = slice(side * HALF + row, side * HALF + row + STEP)
                total = inner[group, rows, :] + f32(edge_in[side, group, row : row + STEP, :]) * keeps[side]
                inner[group, rows, :] = total
                gated[group, rows, :] = bf(gelu(total))


def exchange_grads(wide, send, after, before):
    from_after = send(wide.at[1, :, pl.ds(0, HALF)], wide.at[0, :, pl.ds(HALF, HALF)], before)
    from_before = send(wide.at[1, :, pl.ds(HALF, HALF)], wide.at[2, :, pl.ds(0, HALF)], after)
    wide[0, :, 0:HALF, :] = wide[1, :, HALF:128, :]
    wide[2, :, HALF:128, :] = wide[1, :, 0:HALF, :]
    return from_after, from_before


def finish_exchange(wide, copies, seq, groups):
    copies[0].wait_recv()
    copies[1].wait_recv()
    zeros = jnp.zeros((wide.shape[1], HALF, INNER), jnp.bfloat16)

    @pl.when(seq == groups - 1)
    def _():
        wide[0, :, HALF:128, :] = zeros

    @pl.when(seq == 0)
    def _():
        wide[2, :, 0:HALF, :] = zeros


def gradient_rows(transposed, right, store):
    @pl.loop(0, 4)
    def _(y):
        result = dot(transposed[pl.ds(pl.multiple_of(y * 192, 64), 192), :], right())
        for x_hi in range(2):
            for z in range(4):
                row = 24 * (4 * x_hi + z)
                store(y, x_hi, z, bf(result[row : row + 24]))


def step_kernel(
    emb, weights, layout, length_ref, targets, kernels, mixers, readout,
    joined_out, readout_out, woven_out,
    layout_v, emb_v, w_v, total, rows_v, landed, load_sems, a2a_send, a2a_recv, ready,
    kernels_v, mixers_v, readout_v, targets_v, local_sems,
    hid, act1, inner1, gated1, mixed, first, act2, inner2, gated2, second, logits, logit_grad,
    upper, woven, wide2, wide1, lower, act1_t, act2_t, second_t, gated1_t, gated2_t, picks, mixer_right, mixer_grad,
    edge1_out, edge1_in, edge2_out, edge2_in, *rest
):
    terms, parts_scratch, (joined, send_sems, recv_sems) = rest[:N_PARTS], rest[N_PARTS:-3], rest[-3:]
    coords, core = place()
    dp, seq = lax.axis_index("dp"), lax.axis_index("seq")
    groups = lax.axis_size("seq")
    loads = []
    for at, (src, dst) in enumerate(
        (
            (kernels.at[0], kernels_v.at[0]),
            (mixers, mixers_v),
            (kernels.at[1], kernels_v.at[1]),
            (readout, readout_v),
            (targets, targets_v),
            (layout, layout_v),
        )
    ):
        loads.append(pltpu.make_async_copy(src, dst, local_sems.at[at]))
    after, before = (dp, lax.rem(seq + 1, groups)), (dp, lax.rem(seq + groups - 1, groups))
    send = Sender(send_sems, recv_sems)
    parts = []
    for members in GROUPS:
        parts.append([])
        for order, _ in members:
            at = sum(len(group) for group in parts)
            parts[-1].append(Part(order, terms[at], parts_scratch[6 * at : 6 * at + 6], send, coords, core))

    def put(number, unit):
        def store(y, x_hi, z, block):
            spot = (2 * x_hi + unit // 2, y, z)
            start = 0
            for part, (order, width) in zip(parts[number], GROUPS[number]):
                part.terms[unit % 2, spot[order[0]], spot[order[1]], spot[order[2]]] = block[:, start : start + width]
                start += width

        return store

    def each(number, step):
        return [getattr(part, step)() for part in parts[number]]

    def gather_last(number):
        return jnp.concatenate(each(number, "end_last"), axis=1)

    pair_x = (coords[0] + 1 - 2 * lax.rem(coords[0], 2),) + coords[1:]
    partner = device_at(coords, 1 - core)
    group = [partner, device_at(pair_x, core), device_at(pair_x, 1 - core)]

    def meet():
        greet(
            [device_at(moved(coords, axis, k), core) for axis in range(3) for k in (1, 2, 3)]
            + [partner, device_at(pair_x, 1 - core), after, before]
        )
        for k in (1, 2, 3):
            pl.semaphore_signal(
                ready.at[0], inc=1, device_id=device_at(moved(coords, 1, k), core), device_id_type=MESH
            )

    def pass_on():
        for copy in loads:
            copy.start()
        column = lax.broadcasted_iota(jnp.int32, (CH, CH), 1)
        half = jnp.where(column >= INNER, 1, 0)
        column = column - INNER * half
        target_row = column + 12 * lax.shift_right_logical(column * 43691, 19) + 12 * half
        owner = lax.broadcasted_iota(jnp.int32, (CH, CH), 0)
        picks[...] = jnp.where(owner == target_row, 1.0, 0.0).astype(jnp.bfloat16)
        pl.semaphore_wait(ready.at[0], 3)
        pl.semaphore_signal(
            ready.at[1], inc=1, device_id=device_at(moved(coords, 0, 2), core), device_id_type=MESH
        )

    block_copy = project(
        emb, weights, emb_v, w_v, total, rows_v, landed, coords, core, meet, pass_on, load_sems, send, a2a_send, a2a_recv
    )
    length = length_ref[0]

    pl.semaphore_wait(ready.at[1], 1)

    @pl.loop(1, groups)
    def _(off):
        block_copy(off).start()

    landed[seq] = rows_v[seq]

    @pl.loop(1, groups)
    def _(off):
        block_copy(off).wait()

    loads[5].wait()
    here = lax.broadcasted_iota(jnp.int32, (32, 32), 1) == seq
    column = jnp.sum(jnp.where(here, f32(layout_v[...]), 0.0), axis=1, keepdims=True)
    lane = lax.broadcasted_iota(jnp.int32, (32, 512), 1)
    source = lax.broadcasted_iota(jnp.int32, (32, 512), 0) == lax.shift_right_logical(lane, 4)
    slot = jnp.sum(jnp.where(source, column, 0.0), axis=0, keepdims=True)
    lane_position = slot * 16.0 + f32(lane[0:1] & 15)

    blocks = flat(landed[...])
    for group_at in range(4):
        spot = 4 * lax.broadcasted_iota(jnp.int32, (128, 512), 0) + group_at
        chosen = (lane_position == f32(spot)) & (spot + seq * 512 < length)
        hid[group_at] = bf(dot(jnp.where(chosen, 1.0, 0.0).astype(jnp.bfloat16), blocks))

    for group_at in range(4):

        def gelu_rows(row, group_at=group_at):
            act1[group_at, pl.ds(row, STEP), :] = bf(gelu(f32(hid[group_at, pl.ds(row, STEP), :])))

        row_blocks(128, STEP, gelu_rows)

    loads[0].wait()
    edges = conv_forward(act1, kernels_v.at[0], inner1, edge1_out, edge1_in, send, after, before, seq, groups)
    act1_t[...] = flat(act1[...]).T
    finish_inner(inner1, gated1, edge1_in, edges, seq, groups)
    loads[1].wait()
    mixed[...] = dot(flat(gated1[...]), mixers_v[0]).reshape(mixed.shape)
    for pair in range(2):

        def pool_rows(row, pair=pair):
            rows = pl.ds(row, STEP)
            total = (f32(hid[2 * pair, rows, :]) + mixed[2 * pair, rows, :]) + (
                f32(hid[2 * pair + 1, rows, :]) + mixed[2 * pair + 1, rows, :]
            )
            pooled = bf(total * 0.5)
            first[pair, rows, :] = pooled
            act2[pair, rows, :] = bf(gelu(f32(pooled)))

        row_blocks(128, STEP, pool_rows)

    loads[2].wait()
    edges = conv_forward(act2, kernels_v.at[1], inner2, edge2_out, edge2_in, send, after, before, seq, groups)
    act2_t[...] = flat(act2[...]).T
    gated1_t[...] = flat(gated1[...]).T
    finish_inner(inner2, gated2, edge2_in, edges, seq, groups)
    mixed[0:2] = dot(flat(gated2[...]), mixers_v[1]).reshape(2, 128, CH)

    def pool_again(row):
        rows = pl.ds(row, STEP)
        total = (f32(first[0, rows, :]) + mixed[0, rows, :]) + (f32(first[1, rows, :]) + mixed[1, rows, :])
        second[rows, :] = bf(total * 0.5)

    row_blocks(128, STEP, pool_again)
    loads[3].wait()
    loads[4].wait()
    logits[...] = dot(second[...], readout_v[...])
    loss_scale = 2.0 / math.sqrt(lax.axis_size("dp") * groups * 128)

    def loss_rows(row):
        rows = pl.ds(row, 8)
        values = logits[rows, :]
        small = jnp.exp(-jnp.abs(values))
        softplus = jnp.maximum(values, 0.0) + jnp.log1p(small)
        sigmoid = jnp.where(values >= 0.0, 1.0, small) / (1.0 + small)
        bins = seq * 128 + row + lax.broadcasted_iota(jnp.int32, (8, 1), 0)
        valid = jnp.where(bins * 4 < length, loss_scale, 0.0)
        mixed_rows = valid * (softplus - targets_v[rows, :].astype(jnp.float32)) * sigmoid
        logits[rows, :] = mixed_rows

    row_blocks(128, 8, loss_rows)
    logit_grad[...] = bf(logits[...])
    upper[...] = bf(dot_nt(logit_grad[...], readout_v[...]) * 0.5)
    back = dot_nt(upper[...], mixers_v[1])
    logits[:, 0:INNER] = back

    def coarse_rows(row):
        rows = pl.ds(row, STEP)
        back_rows = logits[rows, 0:INNER]
        for pair in range(2):
            wide2[1, pair, rows, :] = bf(back_rows * gelu_slope(inner2[pair, rows, :]))

    row_blocks(128, STEP, coarse_rows)
    edges = exchange_grads(wide2, send, after, before)
    second_t[...] = second[...].T
    for index in range(4):
        gradient_rows(second_t, lambda i=index: logit_grad[:, 512 * i : 512 * i + 512], put(2, index))
    each(2, "start_pair")
    gradient_rows(act2_t, lambda: flat(wide2[1]), put(1, 1))

    def mixer_gradient(gated_t, right, store):
        total = dot(gated_t[...], right)
        mixer_grad[0:INNER] = bf(total[:, 0:INNER])
        mixer_grad[INNER:CH] = bf(total[:, INNER:CH])
        gradient_rows(picks, lambda: mixer_grad[...], store)

    gated2_t[...] = flat(gated2[...]).T
    for pair in range(2):
        mixer_right[128 * pair : 128 * pair + 128] = upper[...]
    mixer_gradient(gated2_t, mixer_right[0:256], put(1, 3))
    each(2, "start_first")
    finish_exchange(wide2, edges, seq, groups)
    gradient_rows(act2_t, lambda: flat(wide2[0]), put(1, 0))
    gradient_rows(act2_t, lambda: flat(wide2[2]), put(1, 2))
    each(1, "start_pair")
    mixed[0:2] = (
        dot_nt(flat(wide2[0]), kernels_v[1, 0])
        + dot_nt(flat(wide2[1]), kernels_v[1, 1])
        + dot_nt(flat(wide2[2]), kernels_v[1, 2])
    ).reshape(2, 128, CH)
    trunk_scale = math.sqrt(lax.axis_size("dp") * groups * 128) * 0.5

    def trunk_rows(row):
        rows = pl.ds(row, STEP)
        upper_rows = f32(upper[rows, :])
        for pair in range(2):
            grad = upper_rows + mixed[pair, rows, :] * gelu_slope(f32(first[pair, rows, :]))
            scaled = grad * trunk_scale
            for at in range(6):
                woven[at, pl.ds(2 * row + pair, STEP, stride=2), :] = scaled[:, 128 * at : 128 * at + 128]
            lower[pair, rows, :] = bf(grad * 0.5)

    row_blocks(128, STEP, trunk_rows)
    woven_copy = pltpu.make_async_copy(woven, woven_out, local_sems.at[6])
    woven_copy.start()
    each(2, "relay_first")
    each(1, "start_first")
    back = dot_nt(flat(lower[...]), mixers_v[0])
    mixed[0:2, :, 0:INNER] = back.reshape(2, 128, INNER)
    for pair in range(2):

        def fine_rows(row, pair=pair):
            rows = pl.ds(row, STEP)
            back_rows = mixed[pair, rows, 0:INNER]
            for side in range(2):
                wide1[1, 2 * pair + side, rows, :] = bf(back_rows * gelu_slope(inner1[2 * pair + side, rows, :]))

        row_blocks(128, STEP, fine_rows)

    edges = exchange_grads(wide1, send, after, before)
    each(2, "end_first")
    each(1, "relay_first")
    gradient_rows(act1_t, lambda: flat(wide1[1]), put(0, 1))
    for group_at in range(4):
        mixer_right[128 * group_at : 128 * group_at + 128] = lower[group_at // 2]
    mixer_gradient(gated1_t, mixer_right[...], put(0, 3))
    each(1, "end_first")
    finish_exchange(wide1, edges, seq, groups)
    gradient_rows(act1_t, lambda: flat(wide1[0]), put(0, 0))
    gradient_rows(act1_t, lambda: flat(wide1[2]), put(0, 2))
    each(0, "start_pair")
    each(2, "end_second")
    each(1, "end_second")
    each(0, "start_first")
    readout_out[...] = gather_last(2)
    each(0, "relay_first")
    joined[dp, :, 384:768] = gather_last(1)
    each(0, "end_first")
    each(0, "end_second")
    joined[dp, :, 0:384] = gather_last(0)
    mine = joined.at[dp]
    last = [send(mine, mine, device) for device in group]
    for copy in last:
        copy.wait_recv()
    woven_copy.wait()
    joined_out[...] = joined[...]
    send.finish()


N_PARTS = sum(len(group) for group in GROUPS)
N_GATHER = 8 + 4 + 1 + 24 + 16 + 4
N_COPIES = N_GATHER + N_PARTS * (1 + 6 + 3 + 3) + 3 + 8


def finish_kernel(joined, readout_part, woven, kernel_out, mixer_out, readout_out, trunk_out):
    dp = lax.axis_index("dp")
    for index in range(4):

        @pl.when(dp == index)
        def _():
            low = 96 * index
            for tap in range(6):
                start = 384 * (tap // 3) + low
                kernel_out[tap // 3, tap % 3] = joined[tap % 3, :, start : start + 96]
            row, low = 12 * (index // 2), 192 * (index % 2)
            for block in range(2):
                start = 384 * block + low
                mixer_out[:, block, :] = joined[3, row : row + 12, start : start + 192]

    readout_out[...] = readout_part[...]
    for at in range(6):
        trunk_out[:, 128 * at : 128 * at + 128] = woven[at]


def write_outputs(joined, readout_part, woven):
    vmem, single = pl.BlockSpec(memory_space=pltpu.VMEM), jnp.float32
    return pl.pallas_call(
        finish_kernel,
        out_shape=(
            jax.ShapeDtypeStruct((2, 3, 24, 96), single),
            jax.ShapeDtypeStruct((12, 2, 192), single),
            jax.ShapeDtypeStruct((24, 512), single),
            jax.ShapeDtypeStruct((256, CH), single),
        ),
        in_specs=[vmem] * 3,
        out_specs=[vmem] * 4,
        name="outputs",
    )(joined, readout_part, woven)


def step(emb, weights, layout, length, targets, kernels, mixers, readout):
    vmem, anywhere = pl.BlockSpec(memory_space=pltpu.VMEM), pl.BlockSpec(memory_space=pl.ANY)
    bf16, single = jnp.bfloat16, jnp.float32
    rows, depth, groups = emb.shape[0], weights.shape[0], lax.axis_size("seq")
    blocks = (groups, rows // groups, CH)
    return pl.pallas_call(
        step_kernel,
        out_shape=(
            jax.ShapeDtypeStruct((4, 24, CH), single),
            jax.ShapeDtypeStruct((24, 512), single),
            jax.ShapeDtypeStruct((6, 256, 128), single),
        ),
        in_specs=[anywhere] * 3 + [pl.BlockSpec(memory_space=pltpu.SMEM)] + [anywhere] * 4,
        out_specs=[vmem, vmem, anywhere],
        scratch_shapes=[
            pltpu.VMEM((groups, groups), jnp.int32),
            pltpu.VMEM((2, rows, depth), bf16),
            pltpu.VMEM((4, depth, CH), bf16),
            pltpu.VMEM((rows, CH), single),
            pltpu.VMEM(blocks, bf16),
            pltpu.VMEM(blocks, bf16),
            pltpu.SemaphoreType.DMA((5,)),
            pltpu.SemaphoreType.DMA((groups,)),
            pltpu.SemaphoreType.DMA((groups,)),
            pltpu.SemaphoreType.REGULAR((2,)),
            pltpu.VMEM((2, 3, CH, INNER), bf16),
            pltpu.VMEM((2, INNER, CH), bf16),
            pltpu.VMEM((CH, 2048), bf16),
            pltpu.VMEM((128, 2048), jnp.int32),
            pltpu.SemaphoreType.DMA((7,)),
            pltpu.VMEM((4, 128, CH), bf16),
            pltpu.VMEM((4, 128, CH), bf16),
            pltpu.VMEM((4, 128, INNER), single),
            pltpu.VMEM((4, 128, INNER), bf16),
            pltpu.VMEM((4, 128, CH), single),
            pltpu.VMEM((2, 128, CH), bf16),
            pltpu.VMEM((2, 128, CH), bf16),
            pltpu.VMEM((2, 128, INNER), single),
            pltpu.VMEM((2, 128, INNER), bf16),
            pltpu.VMEM((128, CH), bf16),
            pltpu.VMEM((128, 2048), single),
            pltpu.VMEM((128, 2048), bf16),
            pltpu.VMEM((128, CH), bf16),
            pltpu.VMEM((6, 256, 128), single),
            pltpu.VMEM((3, 2, 128, INNER), bf16),
            pltpu.VMEM((3, 4, 128, INNER), bf16),
            pltpu.VMEM((2, 128, CH), bf16),
            pltpu.VMEM((CH, 512), bf16),
            pltpu.VMEM((CH, 256), bf16),
            pltpu.VMEM((CH, 128), bf16),
            pltpu.VMEM((INNER, 512), bf16),
            pltpu.VMEM((INNER, 256), bf16),
            pltpu.VMEM((CH, CH), bf16),
            pltpu.VMEM((512, CH), bf16),
            pltpu.VMEM((CH, INNER), bf16),
            pltpu.VMEM((2, 4, HALF, INNER), bf16),
            pltpu.VMEM((2, 4, HALF, INNER), bf16),
            pltpu.VMEM((2, 2, HALF, INNER), bf16),
            pltpu.VMEM((2, 2, HALF, INNER), bf16),
        ]
        + [pltpu.VMEM((2, 4, 4, 4, 24, width), bf16) for group in GROUPS for _, width in group]
        + [s for group in GROUPS for _, width in group for s in part_scratch(width)]
        + [
            pltpu.VMEM((4, 24, CH), single),
            pltpu.SemaphoreType.DMA((N_COPIES,)),
            pltpu.SemaphoreType.DMA((N_COPIES,)),
        ],
        compiler_params=pltpu.CompilerParams(
            collective_id=0, has_side_effects=True, vmem_limit_bytes=66 * 10**6
        ),
        name="step",
    )(emb, weights, layout, length, targets, kernels, mixers, readout)


def shards(embeddings, layout, lengths, targets, projection, kernels, mixers, readout):
    kernel_total, mixer_total, readout_total, trunk_grad = write_outputs(
        *step(embeddings[0, 0], projection, layout[0], lengths, targets[0], kernels, mixers, readout)
    )
    return (kernel_total, mixer_total.transpose(1, 0, 2), readout_total, trunk_grad[None])


def solution(mesh):
    placed = (
        P("dp", "seq", None, None),
        P("dp", None, None),
        P("dp"),
        P("dp", "seq", None),
        P("dp", None),
        P(),
        P(),
        P(),
    )
    return jax.shard_map(
        shards,
        mesh=mesh,
        in_specs=placed,
        out_specs=(
            P(None, None, "seq", "dp"),
            P(None, "seq", "dp"),
            P("seq", "dp"),
            P("dp", "seq", None),
        ),
        check_vma=False,
    )
```

```python
import math

import jax
import jax.numpy as jnp
from jax import lax
from jax.experimental import pallas as pl
from jax.experimental.pallas import tpu as pltpu
from jax.sharding import PartitionSpec as P

MESH = pl.DeviceIdType.MESH
CHUNK = 512
STAGES = ((0, 512, 96), (1280, 256, 64))
STAGE_ROWS = (1280, 768)
GROUPS = (
    (((0, 1, 2), 128), ((1, 2, 0), 128), ((2, 0, 1), 128)),
    (((0, 1, 2), 128), ((1, 2, 0), 128), ((2, 0, 1), 128)),
    (((1, 0, 2), 256), ((0, 1, 2), 256)),
)


def place():
    dp, seq = lax.axis_index("dp"), lax.axis_index("seq")
    core = lax.rem(dp, 2)
    x = lax.rem(lax.div(seq, 4), 2) * 2 + lax.div(dp, 2)
    return (x, lax.div(seq, 8), lax.rem(seq, 4)), core


def device_at(coords, core):
    x, y, z = coords
    return (lax.rem(x, 2) * 2 + core, y * 8 + lax.div(x, 2) * 4 + z)


def moved(coords, axis, step):
    out = list(coords)
    out[axis] = lax.rem(out[axis] + step, 4)
    return tuple(out)


class Sender:
    def __init__(self, send_sems, recv_sems):
        self.send_sems, self.recv_sems, self.copies = send_sems, recv_sems, []

    def __call__(self, src, dst, device):
        at = len(self.copies)
        copy = pltpu.make_async_remote_copy(
            src_ref=src,
            dst_ref=dst,
            send_sem=self.send_sems.at[at],
            recv_sem=self.recv_sems.at[at],
            device_id=device,
            device_id_type=MESH,
        )
        copy.start()
        self.copies.append(copy)
        return copy

    def finish(self):
        for copy in self.copies:
            copy.wait_send()


def greet(devices):
    barrier = pltpu.get_barrier_semaphore()
    for device in devices:
        pl.semaphore_signal(barrier, inc=1, device_id=device, device_id_type=MESH)
    pl.semaphore_wait(barrier, len(devices))


def f32(values):
    return values.astype(jnp.float32)


def project(emb, weights, emb_v, w_v, acc, rows_v, landed, coords, core, meet, pass_on, local_sems, send, a2a_send, a2a_recv):
    dp, seq = lax.axis_index("dp"), lax.axis_index("seq")
    groups = lax.axis_size("seq")
    depth = weights.shape[0]
    partner = device_at(coords, 1 - core)
    sides = (device_at(moved(coords, 0, 1), core), device_at(moved(coords, 0, 3), core))
    across = lax.rem(dp + 2, 4)
    order = (dp, dp + 1 - 2 * core, across, across + 1 - 2 * core)
    own_w = pltpu.make_async_copy(weights, w_v.at[dp], local_sems.at[4])
    own_w.start()

    def load(at):
        cols = pl.ds(pl.multiple_of(order[at] * depth, depth), depth)
        copy = pltpu.make_async_copy(emb.at[:, cols], emb_v.at[at % 2], local_sems.at[at])
        copy.start()
        return copy

    loads = [load(0), load(1)]
    meet()

    def piece(stage, axis, owner, side):
        base, direct, size = STAGES[stage]
        start = base + direct + 4 * size * (axis - 1)
        if side is None:
            return pl.ds(pl.multiple_of(start + size * owner, 32), size)
        return pl.ds(pl.multiple_of(start + size * owner + size // 2 * side, 16), size // 2)

    def straight(stage, side):
        base, direct, _ = STAGES[stage]
        return pl.ds(base + direct // 2 * side, direct // 2)

    crossing, direct = {}, {}
    for stage in range(2):
        for axis in (1, 2):
            for side in range(2):
                rows = piece(stage, axis, coords[axis], side)
                crossing[stage, axis, side] = send(weights.at[rows], w_v.at[dp, rows], sides[side])
    for stage in range(2):
        for side in range(2):
            rows = straight(stage, side)
            direct[stage, side] = send(weights.at[rows], w_v.at[dp, rows], sides[side])
    to_partner = send(weights, w_v.at[dp], partner)

    def accumulate(at, row, size):
        acc[...] += jnp.dot(
            emb_v[at % 2, :, pl.ds(pl.multiple_of(row, 128), size)],
            w_v[order[at], pl.ds(pl.multiple_of(row, 128), size), :],
            preferred_element_type=jnp.float32,
        )

    rings, relays = {}, {}

    def spread(stage):
        for axis in (1, 2):
            for side in range(2):
                crossing[stage, axis, side].wait_recv()
                block = w_v.at[across, piece(stage, axis, coords[axis], side)]
                for k in (2, 1, 3):
                    rings.setdefault((stage, axis, k), []).append(
                        send(block, block, device_at(moved(coords, axis, k), core))
                    )

    def relay(stage, axis, k):
        block = w_v.at[across, piece(stage, axis, lax.rem(coords[axis] + 4 - k, 4), None)]
        relays[stage, axis, k] = send(block, block, partner)

    def collect(stage):
        for axis in (1, 2):
            relay(stage, axis, 0)
        for side in range(2):
            direct[stage, side].wait_recv()
            block = w_v.at[across, straight(stage, side)]
            relays[stage, 0, side] = send(block, block, partner)
        for k in (1, 3, 2):
            for axis in (1, 2):
                for copy in rings[stage, axis, k]:
                    copy.wait_recv()
                relay(stage, axis, k)

    def take(stage):
        for key, copy in relays.items():
            if key[0] == stage:
                copy.wait_recv()

    acc[...] = jnp.zeros_like(acc)
    loads[0].wait()
    own_w.wait()

    @pl.loop(0, depth // CHUNK)
    def _(step):
        accumulate(0, step * CHUNK, CHUNK)

    loads.append(load(2))
    spread(0)
    pass_on()
    loads[1].wait()
    to_partner.wait_recv()
    accumulate(1, 0, 1024)
    spread(1)
    accumulate(1, 1024, 1024)
    loads.append(load(3))
    loads[2].wait()
    collect(0)
    accumulate(2, 0, STAGE_ROWS[0])
    loads[3].wait()
    take(0)
    accumulate(3, 0, STAGE_ROWS[0])
    collect(1)
    accumulate(2, STAGE_ROWS[0], STAGE_ROWS[1])
    take(1)

    def block_copy(off):
        there = lax.rem(seq + off, groups)
        return pltpu.make_async_remote_copy(
            src_ref=rows_v.at[there],
            dst_ref=landed.at[seq],
            send_sem=a2a_send.at[off],
            recv_sem=a2a_recv.at[off],
            device_id=(dp, there),
            device_id_type=MESH,
        )

    tail = pl.ds(STAGE_ROWS[0], STAGE_ROWS[1])
    total = acc[...] + jnp.dot(emb_v[1, :, tail], w_v[order[3], tail, :], preferred_element_type=jnp.float32)
    rows_v[...] = total.astype(jnp.bfloat16).reshape(rows_v.shape)
    return block_copy


class Part:
    def __init__(self, order, terms, scratch, send, coords, core):
        self.order, self.terms, self.send, self.coords, self.core = order, terms, send, coords, core
        self.pair, self.halves, self.acc2, self.next, self.acc3, self.last = scratch
        self.acc1 = self.pair

    def start_pair(self):
        self.pair_copy = self.send(
            self.terms.at[1 - self.core], self.pair, device_at(self.coords, 1 - self.core)
        )

    def start_first(self):
        self.pair_copy.wait_recv()

        @pl.loop(0, 4)
        def _(at):
            self.acc1[at] = self.terms[self.core, at] + self.pair[at]

        acc, halves = self.acc1, self.halves
        here = self.coords[self.order[0]]
        self.up, self.down = (device_at(moved(self.coords, self.order[0], k), self.core) for k in (1, 3))
        after, before, opposite = (lax.rem(here + k, 4) for k in (1, 3, 2))
        low, high = pl.ds(0, 2), pl.ds(2, 2)
        self.arrivals = [
            self.send(acc.at[opposite, low], halves.at[0], self.up),
            self.send(acc.at[opposite, high], halves.at[1], self.down),
            self.send(acc.at[before, low], halves.at[2], self.down),
            self.send(acc.at[after, high], halves.at[3], self.up),
        ]

    def relay_first(self):
        acc, halves, here = self.acc1, self.halves, self.coords[self.order[0]]
        after, before = (lax.rem(here + k, 4) for k in (1, 3))
        self.arrivals[0].wait_recv()
        acc[after, 0:2] = halves[0] + acc[after, 0:2]
        self.arrivals.append(self.send(acc.at[after, pl.ds(0, 2)], halves.at[4], self.up))
        self.arrivals[1].wait_recv()
        acc[before, 2:4] = halves[1] + acc[before, 2:4]
        self.arrivals.append(self.send(acc.at[before, pl.ds(2, 2)], halves.at[5], self.down))

    def end_first(self):
        acc, halves, here = self.acc1, self.halves, self.coords[self.order[0]]
        for copy in self.arrivals[2:]:
            copy.wait_recv()
        self.acc2[0:2] = (f32(acc[here, 0:2]) + f32(halves[2]) + f32(halves[4])).astype(jnp.bfloat16)
        self.acc2[2:4] = (f32(acc[here, 2:4]) + f32(halves[3]) + f32(halves[5])).astype(jnp.bfloat16)
        self.exchange(1, self.acc2, self.next)

    def exchange(self, number, acc, into):
        axis = self.order[number]
        here = self.coords[axis]
        self.arrivals = [
            self.send(
                acc.at[lax.rem(here + k, 4)],
                into.at[k - 1],
                device_at(moved(self.coords, axis, k), self.core),
            )
            for k in (2, 1, 3)
        ]

    def gathered(self, number, acc, into):
        for copy in self.arrivals:
            copy.wait_recv()
        here = self.coords[self.order[number]]
        return (f32(acc[here]) + f32(into[0])) + (f32(into[1]) + f32(into[2]))

    def end_second(self):
        self.acc3[...] = self.gathered(1, self.acc2, self.next).astype(jnp.bfloat16)
        self.exchange(2, self.acc3, self.last)

    def end_last(self):
        return self.gathered(2, self.acc3, self.last)


class TailPart(Part):
    def exchange(self, number, acc, into):
        if number < 2:
            return Part.exchange(self, number, acc, into)
        axis, (x, y, z), core = self.order[2], self.coords, self.core
        x_hi, x_lo = lax.div(x, 2), lax.rem(x, 2)
        self.arrivals = []
        for other_lo in range(2):
            there_lo = x_lo if other_lo == 0 else 1 - x_lo
            for other_core in range(2):
                there_core = core if other_core == 0 else 1 - core
                for k in range(2 if axis == 0 else 4):
                    if other_lo + other_core + k == 0:
                        continue
                    if axis == 0:
                        there_hi = x_hi if k == 0 else 1 - x_hi
                        block = acc.at[pl.ds(2 * there_hi, 2)]
                        slot, device = into.at[x, core], device_at((2 * there_hi + there_lo, y, z), there_core)
                    else:
                        coords = moved((2 * x_hi + there_lo, y, z), axis, k)
                        block = acc.at[coords[axis]]
                        slot = into.at[self.coords[axis], x_lo, core]
                        device = device_at(coords, there_core)
                    self.arrivals.append(self.send(block, slot, device))
        if axis == 0:
            into[x, core] = acc[pl.ds(2 * x_hi, 2)]
        else:
            here = self.coords[axis]
            into[here, x_lo, core] = acc[here]

    def units(self):
        for copy in self.arrivals:
            copy.wait_recv()
        if self.order[2] == 0:
            return [sum(f32(self.last[x, core, lo]) for x in range(4)) for lo in range(2) for core in range(2)]
        return [sum(f32(self.last[at, lo, core]) for at in range(4)) for lo in range(2) for core in range(2)]


def part_scratch(width, tail):
    unit = (24, width)
    return [
        pltpu.VMEM(shape + unit, jnp.bfloat16)
        for shape in ((4, 4, 4), (6, 2, 4), (4, 4), (3, 4), (4,), (4, 2, 2) if tail else (3,))
    ]


def gelu(values):
    return 0.5 * values * (1.0 + lax.erf(values * (1.0 / math.sqrt(2.0))))


def gelu_slope(values):
    cumulative = 0.5 * (1.0 + lax.erf(values * (1.0 / math.sqrt(2.0))))
    density = jnp.exp(-0.5 * values * values) * (1.0 / math.sqrt(2.0 * math.pi))
    return cumulative + values * density


def bf(values):
    return values.astype(jnp.bfloat16)


def dot(left, right):
    return jnp.dot(left, right, preferred_element_type=jnp.float32)


def dot_nt(left, right):
    return lax.dot_general(
        left, right, (((1,), (1,)), ((), ())), preferred_element_type=jnp.float32
    )


def flat(values):
    return values.reshape(-1, values.shape[-1])


def row_blocks(count, step, body):
    @pl.loop(0, count // step)
    def _(at):
        body(pl.multiple_of(at * step, step))


STEP = 16
HALF = 64
INNER = 384
CH = 768


def conv_forward(act, kernel, inner, edge_out, edge_in, send, after, before, seq, groups):
    low, high = flat(act[:, 0:HALF, :]), flat(act[:, HALF:128, :])
    shape = (act.shape[0], HALF, INNER)
    edge_out[0] = bf(dot(high, kernel[0])).reshape(shape)
    from_before = send(edge_out.at[0], edge_in.at[0], after)
    edge_out[1] = bf(dot(low, kernel[2])).reshape(shape)
    from_after = send(edge_out.at[1], edge_in.at[1], before)
    inner[:, 0:HALF, :] = (dot(low, kernel[1]) + dot(high, kernel[2])).reshape(shape)
    inner[:, HALF:128, :] = (dot(high, kernel[1]) + dot(low, kernel[0])).reshape(shape)
    return from_before, from_after


def finish_inner(inner, gated, edge_in, copies, seq, groups):
    copies[0].wait_recv()
    copies[1].wait_recv()
    keeps = (jnp.where(seq == 0, 0.0, 1.0), jnp.where(seq == groups - 1, 0.0, 1.0))
    for side in range(2):

        @pl.loop(0, inner.shape[0])
        def _(group):
            for row in range(0, HALF, STEP):
                rows = slice(side * HALF + row, side * HALF + row + STEP)
                total = inner[group, rows, :] + f32(edge_in[side, group, row : row + STEP, :]) * keeps[side]
                inner[group, rows, :] = total
                gated[group, rows, :] = bf(gelu(total))


def exchange_grads(wide, send, after, before):
    from_after = send(wide.at[1, :, pl.ds(0, HALF)], wide.at[0, :, pl.ds(HALF, HALF)], before)
    from_before = send(wide.at[1, :, pl.ds(HALF, HALF)], wide.at[2, :, pl.ds(0, HALF)], after)
    wide[0, :, 0:HALF, :] = wide[1, :, HALF:128, :]
    wide[2, :, HALF:128, :] = wide[1, :, 0:HALF, :]
    return from_after, from_before


def finish_exchange(wide, copies, seq, groups):
    copies[0].wait_recv()
    copies[1].wait_recv()
    zeros = jnp.zeros((wide.shape[1], HALF, INNER), jnp.bfloat16)

    @pl.when(seq == groups - 1)
    def _():
        wide[0, :, HALF:128, :] = zeros

    @pl.when(seq == 0)
    def _():
        wide[2, :, 0:HALF, :] = zeros


def gradient_rows(transposed, right, store):
    @pl.loop(0, 4)
    def _(y):
        result = dot(transposed[pl.ds(pl.multiple_of(y * 192, 64), 192), :], right())
        for x_hi in range(2):
            for z in range(4):
                row = 24 * (4 * x_hi + z)
                store(y, x_hi, z, bf(result[row : row + 24]))


def step_kernel(
    emb, weights, layout, length_ref, targets, kernels, mixers, readout,
    joined_out, readout_out, woven_out,
    layout_v, emb_v, w_v, total, rows_v, landed, load_sems, a2a_send, a2a_recv, ready,
    kernels_v, mixers_v, readout_v, targets_v, local_sems,
    hid, act1, inner1, gated1, mixed, first, act2, inner2, gated2, second, logits, logit_grad,
    upper, woven, wide2, wide1, lower, act1_t, act2_t, second_t, gated1_t, gated2_t, picks, mixer_right, mixer_grad,
    edge1_out, edge1_in, edge2_out, edge2_in, *rest
):
    terms, parts_scratch, (joined, send_sems, recv_sems) = rest[:N_PARTS], rest[N_PARTS:-3], rest[-3:]
    coords, core = place()
    dp, seq = lax.axis_index("dp"), lax.axis_index("seq")
    groups = lax.axis_size("seq")
    loads = []
    for at, (src, dst) in enumerate(
        (
            (kernels.at[0], kernels_v.at[0]),
            (mixers, mixers_v),
            (kernels.at[1], kernels_v.at[1]),
            (readout, readout_v),
            (targets, targets_v),
            (layout, layout_v),
        )
    ):
        loads.append(pltpu.make_async_copy(src, dst, local_sems.at[at]))
    after, before = (dp, lax.rem(seq + 1, groups)), (dp, lax.rem(seq + groups - 1, groups))
    send = Sender(send_sems, recv_sems)
    parts = []
    for members in GROUPS:
        parts.append([])
        for order, _ in members:
            at = sum(len(group) for group in parts)
            kind = TailPart if len(parts) == 1 else Part
            parts[-1].append(kind(order, terms[at], parts_scratch[6 * at : 6 * at + 6], send, coords, core))

    def put(number, unit):
        def store(y, x_hi, z, block):
            spot = (2 * x_hi + unit // 2, y, z)
            start = 0
            for part, (order, width) in zip(parts[number], GROUPS[number]):
                part.terms[unit % 2, spot[order[0]], spot[order[1]], spot[order[2]]] = block[:, start : start + width]
                start += width

        return store

    def each(number, step):
        return [getattr(part, step)() for part in parts[number]]

    def gather_last(number):
        return jnp.concatenate(each(number, "end_last"), axis=1)

    pair_x = (coords[0] + 1 - 2 * lax.rem(coords[0], 2),) + coords[1:]
    partner = device_at(coords, 1 - core)
    group = [partner, device_at(pair_x, core), device_at(pair_x, 1 - core)]

    def meet():
        greet(
            [device_at(moved(coords, axis, k), core) for axis in range(3) for k in (1, 2, 3)]
            + [partner, device_at(pair_x, 1 - core), after, before]
        )
        for k in (1, 2, 3):
            pl.semaphore_signal(
                ready.at[0], inc=1, device_id=device_at(moved(coords, 1, k), core), device_id_type=MESH
            )

    def pass_on():
        for copy in loads:
            copy.start()
        column = lax.broadcasted_iota(jnp.int32, (CH, CH), 1)
        half = jnp.where(column >= INNER, 1, 0)
        column = column - INNER * half
        target_row = column + 12 * lax.shift_right_logical(column * 43691, 19) + 12 * half
        owner = lax.broadcasted_iota(jnp.int32, (CH, CH), 0)
        picks[...] = jnp.where(owner == target_row, 1.0, 0.0).astype(jnp.bfloat16)
        pl.semaphore_wait(ready.at[0], 3)
        pl.semaphore_signal(
            ready.at[1], inc=1, device_id=device_at(moved(coords, 0, 2), core), device_id_type=MESH
        )

    block_copy = project(
        emb, weights, emb_v, w_v, total, rows_v, landed, coords, core, meet, pass_on, load_sems, send, a2a_send, a2a_recv
    )
    length = length_ref[0]

    pl.semaphore_wait(ready.at[1], 1)

    @pl.loop(1, groups)
    def _(off):
        block_copy(off).start()

    landed[seq] = rows_v[seq]

    @pl.loop(1, groups)
    def _(off):
        block_copy(off).wait()

    loads[5].wait()
    here = lax.broadcasted_iota(jnp.int32, (32, 32), 1) == seq
    column = jnp.sum(jnp.where(here, f32(layout_v[...]), 0.0), axis=1, keepdims=True)
    lane = lax.broadcasted_iota(jnp.int32, (32, 512), 1)
    source = lax.broadcasted_iota(jnp.int32, (32, 512), 0) == lax.shift_right_logical(lane, 4)
    slot = jnp.sum(jnp.where(source, column, 0.0), axis=0, keepdims=True)
    lane_position = slot * 16.0 + f32(lane[0:1] & 15)

    blocks = flat(landed[...])
    for group_at in range(4):
        spot = 4 * lax.broadcasted_iota(jnp.int32, (128, 512), 0) + group_at
        chosen = (lane_position == f32(spot)) & (spot + seq * 512 < length)
        hid[group_at] = bf(dot(jnp.where(chosen, 1.0, 0.0).astype(jnp.bfloat16), blocks))

    for group_at in range(4):

        def gelu_rows(row, group_at=group_at):
            act1[group_at, pl.ds(row, STEP), :] = bf(gelu(f32(hid[group_at, pl.ds(row, STEP), :])))

        row_blocks(128, STEP, gelu_rows)

    loads[0].wait()
    edges = conv_forward(act1, kernels_v.at[0], inner1, edge1_out, edge1_in, send, after, before, seq, groups)
    act1_t[...] = flat(act1[...]).T
    finish_inner(inner1, gated1, edge1_in, edges, seq, groups)
    loads[1].wait()
    mixed[...] = dot(flat(gated1[...]), mixers_v[0]).reshape(mixed.shape)
    for pair in range(2):

        def pool_rows(row, pair=pair):
            rows = pl.ds(row, STEP)
            total = (f32(hid[2 * pair, rows, :]) + mixed[2 * pair, rows, :]) + (
                f32(hid[2 * pair + 1, rows, :]) + mixed[2 * pair + 1, rows, :]
            )
            pooled = bf(total * 0.5)
            first[pair, rows, :] = pooled
            act2[pair, rows, :] = bf(gelu(f32(pooled)))

        row_blocks(128, STEP, pool_rows)

    loads[2].wait()
    edges = conv_forward(act2, kernels_v.at[1], inner2, edge2_out, edge2_in, send, after, before, seq, groups)
    act2_t[...] = flat(act2[...]).T
    gated1_t[...] = flat(gated1[...]).T
    finish_inner(inner2, gated2, edge2_in, edges, seq, groups)
    mixed[0:2] = dot(flat(gated2[...]), mixers_v[1]).reshape(2, 128, CH)

    def pool_again(row):
        rows = pl.ds(row, STEP)
        total = (f32(first[0, rows, :]) + mixed[0, rows, :]) + (f32(first[1, rows, :]) + mixed[1, rows, :])
        second[rows, :] = bf(total * 0.5)

    row_blocks(128, STEP, pool_again)
    loads[3].wait()
    loads[4].wait()
    logits[...] = dot(second[...], readout_v[...])
    loss_scale = 2.0 / math.sqrt(lax.axis_size("dp") * groups * 128)

    def loss_rows(row):
        rows = pl.ds(row, 8)
        values = logits[rows, :]
        small = jnp.exp(-jnp.abs(values))
        softplus = jnp.maximum(values, 0.0) + jnp.log1p(small)
        sigmoid = jnp.where(values >= 0.0, 1.0, small) / (1.0 + small)
        bins = seq * 128 + row + lax.broadcasted_iota(jnp.int32, (8, 1), 0)
        valid = jnp.where(bins * 4 < length, loss_scale, 0.0)
        mixed_rows = valid * (softplus - targets_v[rows, :].astype(jnp.float32)) * sigmoid
        logits[rows, :] = mixed_rows

    row_blocks(128, 8, loss_rows)
    logit_grad[...] = bf(logits[...])
    upper[...] = bf(dot_nt(logit_grad[...], readout_v[...]) * 0.5)
    back = dot_nt(upper[...], mixers_v[1])
    logits[:, 0:INNER] = back

    def coarse_rows(row):
        rows = pl.ds(row, STEP)
        back_rows = logits[rows, 0:INNER]
        for pair in range(2):
            wide2[1, pair, rows, :] = bf(back_rows * gelu_slope(inner2[pair, rows, :]))

    row_blocks(128, STEP, coarse_rows)
    edges = exchange_grads(wide2, send, after, before)
    second_t[...] = second[...].T
    for index in range(4):
        gradient_rows(second_t, lambda i=index: logit_grad[:, 512 * i : 512 * i + 512], put(2, index))
    each(2, "start_pair")
    gradient_rows(act2_t, lambda: flat(wide2[1]), put(1, 1))

    def mixer_gradient(gated_t, right, store):
        total = dot(gated_t[...], right)
        mixer_grad[0:INNER] = bf(total[:, 0:INNER])
        mixer_grad[INNER:CH] = bf(total[:, INNER:CH])
        gradient_rows(picks, lambda: mixer_grad[...], store)

    gated2_t[...] = flat(gated2[...]).T
    for pair in range(2):
        mixer_right[128 * pair : 128 * pair + 128] = upper[...]
    mixer_gradient(gated2_t, mixer_right[0:256], put(1, 3))
    finish_exchange(wide2, edges, seq, groups)
    each(2, "start_first")
    gradient_rows(act2_t, lambda: flat(wide2[0]), put(1, 0))
    gradient_rows(act2_t, lambda: flat(wide2[2]), put(1, 2))
    each(1, "start_pair")
    mixed[0:2] = (
        dot_nt(flat(wide2[0]), kernels_v[1, 0])
        + dot_nt(flat(wide2[1]), kernels_v[1, 1])
        + dot_nt(flat(wide2[2]), kernels_v[1, 2])
    ).reshape(2, 128, CH)
    each(1, "start_first")
    each(2, "relay_first")
    trunk_scale = math.sqrt(lax.axis_size("dp") * groups * 128) * 0.5

    def trunk_rows(row):
        rows = pl.ds(row, STEP)
        upper_rows = f32(upper[rows, :])
        for pair in range(2):
            grad = upper_rows + mixed[pair, rows, :] * gelu_slope(f32(first[pair, rows, :]))
            mixed[2 + pair, rows, :] = grad * trunk_scale
            lower[pair, rows, :] = bf(grad * 0.5)

    row_blocks(128, STEP, trunk_rows)
    each(1, "relay_first")
    back = dot_nt(flat(lower[...]), mixers_v[0])
    mixed[0:2, :, 0:INNER] = back.reshape(2, 128, INNER)
    for pair in range(2):

        def fine_rows(row, pair=pair):
            rows = pl.ds(row, STEP)
            back_rows = mixed[pair, rows, 0:INNER]
            for side in range(2):
                wide1[1, 2 * pair + side, rows, :] = bf(back_rows * gelu_slope(inner1[2 * pair + side, rows, :]))

        row_blocks(128, STEP, fine_rows)

    edges = exchange_grads(wide1, send, after, before)
    each(2, "end_first")
    gradient_rows(act1_t, lambda: flat(wide1[1]), put(0, 1))
    each(1, "end_first")
    for group_at in range(4):
        mixer_right[128 * group_at : 128 * group_at + 128] = lower[group_at // 2]
    mixer_gradient(gated1_t, mixer_right[...], put(0, 3))

    def weave_rows(row):
        for pair in range(2):
            for at in range(6):
                woven[at, pl.ds(2 * row + pair, STEP, stride=2), :] = mixed[
                    2 + pair, pl.ds(row, STEP), 128 * at : 128 * at + 128
                ]

    row_blocks(128, STEP, weave_rows)
    woven_copy = pltpu.make_async_copy(woven, woven_out, local_sems.at[6])
    woven_copy.start()
    finish_exchange(wide1, edges, seq, groups)
    gradient_rows(act1_t, lambda: flat(wide1[0]), put(0, 0))
    gradient_rows(act1_t, lambda: flat(wide1[2]), put(0, 2))
    each(0, "start_pair")
    each(2, "end_second")
    each(1, "end_second")
    each(0, "start_first")
    readout_out[...] = gather_last(2)
    each(0, "relay_first")
    joined[dp, :, 384:768] = gather_last(1)
    mine = joined.at[dp, :, pl.ds(384, 384)]
    last = [send(mine, mine, device) for device in group]
    each(0, "end_first")
    each(0, "end_second")
    for at, part in enumerate(parts[0]):
        for unit, values in enumerate(part.units()):
            joined[unit, :, 128 * at : 128 * at + 128] = values
    for copy in last:
        copy.wait_recv()
    woven_copy.wait()
    joined_out[...] = joined[...]
    send.finish()


N_PARTS = sum(len(group) for group in GROUPS)
N_GATHER = 8 + 4 + 1 + 24 + 16 + 4
N_COPIES = N_GATHER + N_PARTS * (1 + 6 + 3 + 3) + (12 + 12 + 4) + 3 + 8


def finish_kernel(joined, readout_part, woven, kernel_out, mixer_out, readout_out, trunk_out):
    dp = lax.axis_index("dp")
    for index in range(4):

        @pl.when(dp == index)
        def _():
            low = 96 * index
            for tap in range(6):
                start = 384 * (tap // 3) + low
                kernel_out[tap // 3, tap % 3] = joined[tap % 3, :, start : start + 96]
            row, low = 12 * (index // 2), 192 * (index % 2)
            for block in range(2):
                start = 384 * block + low
                mixer_out[:, block, :] = joined[3, row : row + 12, start : start + 192]

    readout_out[...] = readout_part[...]
    for at in range(6):
        trunk_out[:, 128 * at : 128 * at + 128] = woven[at]


def write_outputs(joined, readout_part, woven):
    vmem, single = pl.BlockSpec(memory_space=pltpu.VMEM), jnp.float32
    return pl.pallas_call(
        finish_kernel,
        out_shape=(
            jax.ShapeDtypeStruct((2, 3, 24, 96), single),
            jax.ShapeDtypeStruct((12, 2, 192), single),
            jax.ShapeDtypeStruct((24, 512), single),
            jax.ShapeDtypeStruct((256, CH), single),
        ),
        in_specs=[vmem] * 3,
        out_specs=[vmem] * 4,
        name="outputs",
    )(joined, readout_part, woven)


def step(emb, weights, layout, length, targets, kernels, mixers, readout):
    vmem, anywhere = pl.BlockSpec(memory_space=pltpu.VMEM), pl.BlockSpec(memory_space=pl.ANY)
    bf16, single = jnp.bfloat16, jnp.float32
    rows, depth, groups = emb.shape[0], weights.shape[0], lax.axis_size("seq")
    blocks = (groups, rows // groups, CH)
    return pl.pallas_call(
        step_kernel,
        out_shape=(
            jax.ShapeDtypeStruct((4, 24, CH), single),
            jax.ShapeDtypeStruct((24, 512), single),
            jax.ShapeDtypeStruct((6, 256, 128), single),
        ),
        in_specs=[anywhere] * 3 + [pl.BlockSpec(memory_space=pltpu.SMEM)] + [anywhere] * 4,
        out_specs=[vmem, vmem, anywhere],
        scratch_shapes=[
            pltpu.VMEM((groups, groups), jnp.int32),
            pltpu.VMEM((2, rows, depth), bf16),
            pltpu.VMEM((4, depth, CH), bf16),
            pltpu.VMEM((rows, CH), single),
            pltpu.VMEM(blocks, bf16),
            pltpu.VMEM(blocks, bf16),
            pltpu.SemaphoreType.DMA((5,)),
            pltpu.SemaphoreType.DMA((groups,)),
            pltpu.SemaphoreType.DMA((groups,)),
            pltpu.SemaphoreType.REGULAR((2,)),
            pltpu.VMEM((2, 3, CH, INNER), bf16),
            pltpu.VMEM((2, INNER, CH), bf16),
            pltpu.VMEM((CH, 2048), bf16),
            pltpu.VMEM((128, 2048), jnp.int32),
            pltpu.SemaphoreType.DMA((7,)),
            pltpu.VMEM((4, 128, CH), bf16),
            pltpu.VMEM((4, 128, CH), bf16),
            pltpu.VMEM((4, 128, INNER), single),
            pltpu.VMEM((4, 128, INNER), bf16),
            pltpu.VMEM((4, 128, CH), single),
            pltpu.VMEM((2, 128, CH), bf16),
            pltpu.VMEM((2, 128, CH), bf16),
            pltpu.VMEM((2, 128, INNER), single),
            pltpu.VMEM((2, 128, INNER), bf16),
            pltpu.VMEM((128, CH), bf16),
            pltpu.VMEM((128, 2048), single),
            pltpu.VMEM((128, 2048), bf16),
            pltpu.VMEM((128, CH), bf16),
            pltpu.VMEM((6, 256, 128), single),
            pltpu.VMEM((3, 2, 128, INNER), bf16),
            pltpu.VMEM((3, 4, 128, INNER), bf16),
            pltpu.VMEM((2, 128, CH), bf16),
            pltpu.VMEM((CH, 512), bf16),
            pltpu.VMEM((CH, 256), bf16),
            pltpu.VMEM((CH, 128), bf16),
            pltpu.VMEM((INNER, 512), bf16),
            pltpu.VMEM((INNER, 256), bf16),
            pltpu.VMEM((CH, CH), bf16),
            pltpu.VMEM((512, CH), bf16),
            pltpu.VMEM((CH, INNER), bf16),
            pltpu.VMEM((2, 4, HALF, INNER), bf16),
            pltpu.VMEM((2, 4, HALF, INNER), bf16),
            pltpu.VMEM((2, 2, HALF, INNER), bf16),
            pltpu.VMEM((2, 2, HALF, INNER), bf16),
        ]
        + [pltpu.VMEM((2, 4, 4, 4, 24, width), bf16) for group in GROUPS for _, width in group]
        + [s for at, group in enumerate(GROUPS) for _, width in group for s in part_scratch(width, at == 0)]
        + [
            pltpu.VMEM((4, 24, CH), single),
            pltpu.SemaphoreType.DMA((N_COPIES,)),
            pltpu.SemaphoreType.DMA((N_COPIES,)),
        ],
        compiler_params=pltpu.CompilerParams(
            collective_id=0, has_side_effects=True, vmem_limit_bytes=66 * 10**6
        ),
        name="step",
    )(emb, weights, layout, length, targets, kernels, mixers, readout)


def shards(embeddings, layout, lengths, targets, projection, kernels, mixers, readout):
    kernel_total, mixer_total, readout_total, trunk_grad = write_outputs(
        *step(embeddings[0, 0], projection, layout[0], lengths, targets[0], kernels, mixers, readout)
    )
    return (kernel_total, mixer_total.transpose(1, 0, 2), readout_total, trunk_grad[None])


def solution(mesh):
    placed = (
        P("dp", "seq", None, None),
        P("dp", None, None),
        P("dp"),
        P("dp", "seq", None),
        P("dp", None),
        P(),
        P(),
        P(),
    )
    return jax.shard_map(
        shards,
        mesh=mesh,
        in_specs=placed,
        out_specs=(
            P(None, None, "seq", "dp"),
            P(None, "seq", "dp"),
            P("seq", "dp"),
            P("dp", "seq", None),
        ),
        check_vma=False,
    )
```
